256 devices in a mesh: gx: 4 (over z_hi), gy: 8 (over z_lo, x), gz: 8 (over y, core).
Axes of the slice: x: 4, y: 4, z: 8 (z_hi: 4, z_lo: 2; z = z_hi * 2 + z_lo), core: 2. Of those that a mesh axis runs over, the one named last changes fastest.
Arguments:
- positions: float32 [3, 8, 8, 16, 8], P(None, 'gx', 'gy', 'gz'), as said below
- features: float32 [8, 8, 16, 8, 128], P('gx', 'gy', 'gz'), may hold values from -6 to 6
- species: int32 [8, 8, 16, 8], P('gx', 'gy', 'gz'), may hold values from 0 to 4
- centers: int32 [8192], P(('gx', 'gy', 'gz')), may hold values from 0 to 32, as said below
- neighbours: int32 [8192, 32], P(('gx', 'gy', 'gz')), may hold values from 0 to 384, as said below
- counts: int32 [256], P(('gx', 'gy', 'gz')), may hold values from 0 to 32, as said below
- species_scale: float32 [5], replicated, may hold values from 0.5 to 2
- species_shift: float32 [5], replicated, may hold values from -4 to 4
- center_weight: float32 [128, 128], replicated, may hold values from -0.5 to 0.5
- near_weight: float32 [128, 128], replicated, may hold values from -0.5 to 0.5
- basis_weight: float32 [8, 128], replicated, may hold values from -12 to 12
- path_weight: float32 [3, 128], replicated, may hold values from -6 to 6
- value_weight: float32 [128, 256], replicated, may hold values from -0.5 to 0.5
- latent_weight: float32 [256, 128], replicated, may hold values from -0.375 to 0.375
- out_weight: float32 [128], replicated, may hold values from -0.5 to 0.5
Outputs:
- site_energy: float32 [8, 8, 16, 8], P('gx', 'gy', 'gz')
- forces: float32 [3, 8, 8, 16, 8], P(None, 'gx', 'gy', 'gz')
- virial: float32 [9, 8, 8, 16, 8], P(None, 'gx', 'gy', 'gz')
The draws below stay inside these ranges and needn't reach their ends.
Inputs may be any that keep to these rules, and one draw needn't show every extreme that they name: `positions`: a listed neighbour lies within two lattice steps of its center, closer than 4.95 Angstrom; coordinates are the site's place in the cell plus a small jitter. `centers`: domain d's block of 32 entries lists its occupied own slots in increasing order, then 32 in the rest. `neighbours`: row k of domain d's block holds the frame rows of the occupied sites within two lattice steps of center k, in any order, and 384 in the other entries; rows of padding centers are all 384. counts[d] is the number of entries of domain d's block of centers that are not 32; some domain holds 32.
All inputs are finite; a program needn't handle non-finite values.
Results may differ from the reference program's by a relative error of at most 0.0003.
Values sent between devices are 32-bit elements; how exact they have to be, the bound alone decides.
A program may use at most 64 MiB of HBM per device.

```python
import math
import jax
import jax.numpy as jnp
import numpy as np
from jax import lax

C = 128
NB = 8
NSPEC = 5
SLOT = 8
NBR = 32
CX = 2
CY = 1
CZ = 2
DOMS_X = 4
DOMS_Y = 8
DOMS_Z = 8
DOMAINS = 256
NCX = 8
NCY = 8
NCZ = 16
OWN = 32
FRAME = 384


def lattice_offsets():
    table = []
    for step_x in range(-2, 3):
        for step_y in range(-2, 3):
            for step_z in range(-2, 3):
                radius = step_x * step_x + step_y * step_y + step_z * step_z
                if 0 < radius <= 4:
                    table.append([step_x, step_y, step_z])
    return np.array(table, dtype=np.int32)


def lattice_layout(key):
    base = jax.random.fold_in(key, 811)
    doms_x = NCX // CX
    doms_y = NCY // CY
    doms_z = NCZ // CZ
    domains = doms_x * doms_y * doms_z
    owned = SLOT * CX * CY * CZ
    frame_count = SLOT * (CX + 2) * (CY + 2) * (CZ + 2)
    order = jnp.arange(domains)
    dense = jax.random.randint(jax.random.fold_in(base, 1), (domains,), 0, 4) == 0
    chosen = jax.random.randint(jax.random.fold_in(base, 2), (), 0, domains)
    dense = jnp.where(order == chosen, True, dense)
    dense = jnp.where(order == (chosen + 1) % domains, False, dense)
    keep = jax.random.randint(jax.random.fold_in(base, 3), (domains, owned), 0, 10) < 8
    keep = keep | dense[:, None]
    counts = jnp.sum(keep.astype(jnp.int32), axis=1)
    slot_ids = jnp.arange(owned)
    score = (1 - keep.astype(jnp.int32)) * owned + slot_ids[None, :]
    ordered = jnp.argsort(score, axis=1)
    centers = jnp.where(slot_ids[None, :] < counts[:, None], ordered, owned).astype(jnp.int32)
    lattice = keep.reshape(doms_x, doms_y, doms_z, CX, CY, CZ, 2, 2, 2)
    lattice = jnp.transpose(lattice, (0, 3, 6, 1, 4, 7, 2, 5, 8)).reshape(2 * NCX, 2 * NCY, 2 * NCZ)
    site = centers % SLOT
    cell = centers // SLOT
    cell_z = cell % CZ
    cell_y = cell // CZ % CY
    cell_x = cell // (CZ * CY)
    local_x = 2 * cell_x + site // 4
    local_y = 2 * cell_y + site // 2 % 2
    local_z = 2 * cell_z + site % 2
    offsets = jnp.asarray(lattice_offsets())
    near_x = local_x[..., None] + offsets[:, 0]
    near_y = local_y[..., None] + offsets[:, 1]
    near_z = local_z[..., None] + offsets[:, 2]
    domain_x = (order // (doms_y * doms_z))[:, None, None]
    domain_y = (order // doms_z % doms_y)[:, None, None]
    domain_z = (order % doms_z)[:, None, None]
    global_x = (domain_x * 2 * CX + near_x) % (2 * NCX)
    global_y = (domain_y * 2 * CY + near_y) % (2 * NCY)
    global_z = (domain_z * 2 * CZ + near_z) % (2 * NCZ)
    occupied = lattice[global_x, global_y, global_z]
    frame_x = near_x + 2
    frame_y = near_y + 2
    frame_z = near_z + 2
    rows = ((frame_x // 2 * (CY + 2) + frame_y // 2) * (CZ + 2) + frame_z // 2) * SLOT
    rows = rows + frame_x % 2 * 4 + frame_y % 2 * 2 + frame_z % 2
    live_center = (slot_ids[None, :] < counts[:, None])[..., None]
    rows = jnp.where(occupied & live_center, rows, frame_count)
    count_slots = offsets.shape[0]
    shuffle = jax.random.randint(jax.random.fold_in(base, 4), (domains, owned, count_slots), 0, 1 << 20) * count_slots + jnp.arange(count_slots)
    arrangement = jnp.argsort(shuffle, axis=-1)
    rows = jnp.take_along_axis(rows, arrangement, axis=-1)
    return (centers.reshape(-1), rows.reshape(domains * owned, count_slots).astype(jnp.int32), counts.astype(jnp.int32))


def draw_centers(key, part):
    return lattice_layout(key)[0]


def draw_neighbours(key, part):
    return lattice_layout(key)[1]


def draw_counts(key, part):
    return lattice_layout(key)[2]


def draw_positions(key, part):
    site = jnp.arange(SLOT)
    sub_cell = jnp.stack([site // 4, site // 2 % 2, site % 2]).astype(jnp.float32)
    centre = (sub_cell + 0.5) * 2.3
    extent = (3, NCX, NCY, NCZ, SLOT)
    jitter = jnp.clip(0.06 * jax.random.normal(key, extent, jnp.float32), -0.15, 0.15)
    return centre[:, None, None, None, :] + jitter


def set_ends(entries, own_key, least, high):
    longest = entries.shape.index(max(entries.shape))
    spots = []
    for shift in (0, 1):
        where = [jax.random.randint(jax.random.fold_in(own_key, axis), (), 0, length) for axis, length in enumerate(entries.shape)]
        where[longest] = (where[longest] + shift) % entries.shape[longest]
        spots.append(tuple(where))
    return entries.at[spots[0]].set(least).at[spots[1]].set(high)


def block_levels(key, shape, shards, least, high):
    level, own = 1.0, jax.random.fold_in(key, 6)
    for position, parts in shards:
        draws = jnp.exp(jax.random.uniform(jax.random.fold_in(own, position), (parts,), jnp.float32, least / len(shards), high / len(shards)))
        level = level * jnp.repeat(draws, shape[position] // parts).reshape([-1 if axis == position else 1 for axis in range(len(shape))])
    return level


def scatter_about(stream_key, shape, scale, bound, split=(), kind=jnp.bfloat16):
    entries = jax.random.normal(stream_key, shape, jnp.float32) * scale
    if len(split) > 0:
        entries = block_levels(stream_key, shape, split, -0.22, 0.18) * entries
    return jnp.clip(entries, min=-bound, max=bound).astype(kind)


def setup_inputs(seed: int = 0) -> dict:
    key_list = jax.random.split(jax.random.key(seed), 16)
    positions = draw_positions(jax.random.fold_in(key_list[15], 71), 0)
    features = scatter_about(key_list[1], (NCX, NCY, NCZ, SLOT, C), 1.0, 6.0, ((0, 4), (1, 8), (2, 8)), jnp.float32)
    species = set_ends(jax.random.randint(key_list[2], (NCX, NCY, NCZ, SLOT), 0, NSPEC), jax.random.fold_in(key_list[2], 1), 0, NSPEC - 1).astype(jnp.int32)
    centers = draw_centers(jax.random.fold_in(key_list[15], 71), 0)
    neighbours = draw_neighbours(jax.random.fold_in(key_list[15], 71), 0)
    counts = draw_counts(jax.random.fold_in(key_list[15], 71), 0)
    species_scale = jnp.clip(jnp.exp(jax.random.uniform(key_list[6], (NSPEC,), jnp.float32, math.log(0.5), math.log(2.0))), 0.5, 2.0)
    species_shift = scatter_about(key_list[7], (NSPEC,), 1.0, 4.0, (), jnp.float32)
    center_weight = scatter_about(key_list[8], (C, C), C ** -0.5, 0.5, (), jnp.float32)
    near_weight = scatter_about(key_list[9], (C, C), C ** -0.5, 0.5, (), jnp.float32)
    basis_weight = scatter_about(key_list[10], (NB, C), 2.0, 12.0, (), jnp.float32)
    path_weight = scatter_about(key_list[11], (3, C), 1.0, 6.0, (), jnp.float32)
    value_weight = scatter_about(key_list[12], (C, 2 * C), C ** -0.5, 0.5, (), jnp.float32)
    latent_weight = scatter_about(key_list[13], (2 * C, C), (2 * C) ** -0.5, 0.375, (), jnp.float32)
    out_weight = scatter_about(key_list[14], (C,), C ** -0.5, 0.5, (), jnp.float32)
    return dict(positions=positions, features=features, species=species, centers=centers, neighbours=neighbours, counts=counts, species_scale=species_scale, species_shift=species_shift, center_weight=center_weight, near_weight=near_weight, basis_weight=basis_weight, path_weight=path_weight, value_weight=value_weight, latent_weight=latent_weight, out_weight=out_weight)


EXACT_DOT = lax.Precision.HIGHEST
CUTOFF = 5.0
CELL_SIDE = 4.6
ROOT_HALF = 0.7071067811865476

def envelope(ratio):
    polynomial = 1.0 - 28.0 * ratio ** 6 + 48.0 * ratio ** 7 - 21.0 * ratio ** 8
    return jnp.where(ratio < 1.0, polynomial, 0.0)

def harmonics(unit):
    along_x = unit[..., 0]
    along_y = unit[..., 1]
    along_z = unit[..., 2]
    root_three = math.sqrt(3.0)
    root_fifteen = math.sqrt(15.0)
    root_five = math.sqrt(5.0)
    return jnp.stack([jnp.ones_like(along_x), root_three * along_x, root_three * along_y, root_three * along_z, root_fifteen * along_x * along_y, root_fifteen * along_y * along_z, 0.5 * root_five * (3.0 * along_z * along_z - 1.0), root_fifteen * along_x * along_z, 0.5 * root_fifteen * (along_x * along_x - along_y * along_y)], axis=-1)

def path_table(path_weight):
    width = path_weight.shape[1]
    return jnp.concatenate([path_weight[0:1], jnp.broadcast_to(path_weight[1:2], (3, width)), jnp.broadcast_to(path_weight[2:3], (5, width))], axis=0)

def center_energy(displace, live, center_proj, near_proj, scale, shift, active, basis_weight, paths, value_weight, latent_weight, out_weight):
    width = center_proj.shape[-1]
    neighbours_count = displace.shape[1]
    length = jnp.sqrt(lax.optimization_barrier(jnp.sum(displace * displace, axis=-1)))
    ratio = length / CUTOFF
    weight = envelope(ratio) * live
    frequency = jnp.arange(1, basis_weight.shape[0] + 1).astype(jnp.float32) * math.pi
    basis = math.sqrt(2.0 / CUTOFF) * jnp.sin(ratio[..., None] * frequency) / length[..., None]
    angular = harmonics(displace / length[..., None])
    radial = jnp.einsum('knb,bc->knc', basis, basis_weight, precision=EXACT_DOT)
    latent = weight[..., None] * jax.nn.silu(radial + center_proj[:, None, :] + near_proj)
    mixed = jnp.einsum('knc,cd->knd', latent, value_weight, precision=EXACT_DOT)
    values = mixed[..., :width]
    env_weight = mixed[..., width:]
    embed = jnp.einsum('knc,knm->kcm', env_weight, angular, precision=EXACT_DOT) / math.sqrt(neighbours_count)
    weighted = embed * jnp.transpose(paths)[None]
    inner = jnp.einsum('knm,kcm->knc', angular, weighted, precision=EXACT_DOT)
    scalars = values * inner
    joined = jnp.concatenate([latent, scalars], axis=-1)
    update = jax.nn.silu(jnp.einsum('knc,cd->knd', joined, latent_weight, precision=EXACT_DOT))
    final = (latent + weight[..., None] * update) * ROOT_HALF
    pair_energy = jnp.einsum('knc,c->kn', final, out_weight, precision=EXACT_DOT)
    return active * (scale * lax.optimization_barrier(jnp.sum(pair_energy, axis=1)) / math.sqrt(neighbours_count) + shift)

def own_to_frame(slots, cells_x, cells_y, cells_z, sites):
    owned = cells_x * cells_y * cells_z * sites
    frame_count = (cells_x + 2) * (cells_y + 2) * (cells_z + 2) * sites
    site = slots % sites
    cell = slots // sites
    cell_z = cell % cells_z
    cell_y = cell // cells_z % cells_y
    cell_x = cell // (cells_z * cells_y)
    frame = (((cell_x + 1) * (cells_y + 2) + cell_y + 1) * (cells_z + 2) + cell_z + 1) * sites + site
    return jnp.where(slots < owned, frame, frame_count).astype(jnp.int32)

def cell_corner(span_x, span_y, span_z):
    grid_x = jnp.broadcast_to(jnp.arange(span_x).astype(jnp.float32)[:, None, None], (span_x, span_y, span_z))
    grid_y = jnp.broadcast_to(jnp.arange(span_y).astype(jnp.float32)[None, :, None], (span_x, span_y, span_z))
    grid_z = jnp.broadcast_to(jnp.arange(span_z).astype(jnp.float32)[None, None, :], (span_x, span_y, span_z))
    return (jnp.stack([grid_x, grid_y, grid_z], axis=-1) * CELL_SIDE)[:, :, :, None, :]

def pair_return(totals, centre_rows, near_rows, displace, pair_grad):
    block = displace.shape[0]
    slots_count = displace.shape[1]
    pair_virial = -(displace[..., :, None] * pair_grad[..., None, :]).reshape(block, slots_count, 9)
    centre_part = jnp.concatenate([lax.optimization_barrier(jnp.sum(pair_grad, axis=1)), 0.5 * lax.optimization_barrier(jnp.sum(pair_virial, axis=1))], axis=-1)
    near_part = jnp.concatenate([-pair_grad, 0.5 * pair_virial], axis=-1).reshape(block * slots_count, 12)
    totals = totals.at[centre_rows].add(centre_part)
    return totals.at[near_rows.reshape(-1)].add(near_part)

def fold_axis(grid, axis, count):
    moved = jnp.moveaxis(grid, axis, 0)
    inner = moved[1:count + 1]
    inner = inner.at[0].add(moved[count + 1])
    inner = inner.at[count - 1].add(moved[0])
    return jnp.moveaxis(inner, 0, axis)

def reference(positions, features, species, centers, neighbours, counts, species_scale, species_shift, center_weight, near_weight, basis_weight, path_weight, value_weight, latent_weight, out_weight):
    width = features.shape[-1]
    flat = features.reshape(-1, width)
    center_all = jnp.dot(flat, center_weight, precision=EXACT_DOT, preferred_element_type=jnp.float32).reshape(NCX, NCY, NCZ, SLOT, width)
    near_all = jnp.dot(flat, near_weight, precision=EXACT_DOT, preferred_element_type=jnp.float32).reshape(NCX, NCY, NCZ, SLOT, width)
    near_pad = jnp.pad(near_all, ((1, 1), (1, 1), (1, 1), (0, 0), (0, 0)), mode='wrap')
    position_pad = jnp.pad(positions, ((0, 0), (1, 1), (1, 1), (1, 1), (0, 0)), mode='wrap')
    paths = path_table(path_weight)
    corner = cell_corner(CX + 2, CY + 2, CZ + 2)
    dead_shift = jnp.array([6.0, 0.0, 0.0], jnp.float32)
    zero_index = jnp.zeros((), jnp.int32)

    def domain(index):
        index = index.astype(jnp.int32)
        start_x = (index // (DOMS_Y * DOMS_Z) * CX).astype(jnp.int32)
        start_y = (index // DOMS_Z % DOMS_Y * CY).astype(jnp.int32)
        start_z = (index % DOMS_Z * CZ).astype(jnp.int32)
        in_cell = lax.dynamic_slice(position_pad, (zero_index, start_x, start_y, start_z, zero_index), (3, CX + 2, CY + 2, CZ + 2, SLOT))
        frame_position = (jnp.transpose(in_cell, (1, 2, 3, 4, 0)) + corner).reshape(FRAME, 3)
        frame_position = jnp.concatenate([frame_position, jnp.zeros((1, 3), jnp.float32)], axis=0)
        near = lax.dynamic_slice(near_pad, (start_x, start_y, start_z, zero_index, zero_index), (CX + 2, CY + 2, CZ + 2, SLOT, width)).reshape(FRAME, width)
        near = jnp.concatenate([near, jnp.zeros((1, width), jnp.float32)], axis=0)
        own_center = lax.dynamic_slice(center_all, (start_x, start_y, start_z, zero_index, zero_index), (CX, CY, CZ, SLOT, width)).reshape(OWN, width)
        own_center = jnp.concatenate([own_center, jnp.zeros((1, width), jnp.float32)], axis=0)
        own_species = lax.dynamic_slice(species, (start_x, start_y, start_z, zero_index), (CX, CY, CZ, SLOT)).reshape(OWN)
        own_species = jnp.concatenate([own_species, jnp.zeros((1,), jnp.int32)], axis=0)
        first = (index * OWN).astype(jnp.int32)
        slots = lax.dynamic_slice(centers, (first,), (OWN,)).astype(jnp.int32)
        rows = lax.dynamic_slice(neighbours, (first, zero_index), (OWN, NBR)).astype(jnp.int32)
        active = (jnp.arange(OWN).astype(jnp.int32) < counts[index]).astype(jnp.float32)
        kind = own_species[slots]
        scale = species_scale[kind]
        shift = species_shift[kind]
        centre_rows = own_to_frame(slots, CX, CY, CZ, SLOT)
        live = (rows != FRAME).astype(jnp.float32)
        separation = frame_position[rows] - frame_position[centre_rows][:, None, :]
        displace = jnp.where(live[..., None] > 0.0, separation, dead_shift)
        center_proj = own_center[slots]
        near_proj = near[rows]

        def energy_of(moved):
            return center_energy(moved, live, center_proj, near_proj, scale, shift, active, basis_weight, paths, value_weight, latent_weight, out_weight)
        energies, pull = jax.vjp(energy_of, displace)
        pair_grad = pull(jnp.ones_like(energies))[0]
        totals = pair_return(jnp.zeros((FRAME + 1, 12), jnp.float32), centre_rows, rows, displace, pair_grad)
        energy = jnp.zeros((OWN + 1,), jnp.float32).at[slots].add(energies)
        return (totals[:FRAME].reshape(CX + 2, CY + 2, CZ + 2, SLOT, 12), energy[:OWN].reshape(CX, CY, CZ, SLOT))
    frames, energies = lax.map(domain, jnp.arange(DOMAINS).astype(jnp.int32))

    def place(index, grid):
        index = jnp.asarray(index).astype(jnp.int32)
        start = ((index // (DOMS_Y * DOMS_Z) * CX).astype(jnp.int32), (index // DOMS_Z % DOMS_Y * CY).astype(jnp.int32), (index % DOMS_Z * CZ).astype(jnp.int32), zero_index, zero_index)
        current = lax.dynamic_slice(grid, start, (CX + 2, CY + 2, CZ + 2, SLOT, 12))
        return lax.dynamic_update_slice(grid, current + frames[index], start)
    grid = lax.fori_loop(0, DOMAINS, place, jnp.zeros((NCX + 2, NCY + 2, NCZ + 2, SLOT, 12), jnp.float32))
    grid = fold_axis(grid, 0, NCX)
    grid = fold_axis(grid, 1, NCY)
    grid = fold_axis(grid, 2, NCZ)
    forces = jnp.transpose(grid[..., 0:3], (4, 0, 1, 2, 3))
    virial = jnp.transpose(grid[..., 3:12], (4, 0, 1, 2, 3))
    site_energy = energies.reshape(DOMS_X, DOMS_Y, DOMS_Z, CX, CY, CZ, SLOT)
    site_energy = jnp.transpose(site_energy, (0, 3, 1, 4, 2, 5, 6)).reshape(NCX, NCY, NCZ, SLOT)
    return (site_energy, forces, virial)
```

```python
import functools
import math

import jax
import jax.numpy as jnp
import numpy as np
from jax import lax
from jax.experimental import pallas as pl
from jax.experimental.pallas import tpu as pltpu
from jax.sharding import PartitionSpec as P

MESH = pl.DeviceIdType.MESH
F32 = jnp.float32
BF16 = jnp.bfloat16
CUTOFF = 5.0
CELL_SIDE = 4.6
ROOT_HALF = 0.7071067811865476
CHANNELS = 128
PAIRS = 1024
DIRECTIONS = [(a, b, c) for a in (-1, 0, 1) for b in (-1, 0, 1) for c in (-1, 0, 1)]
HOME = 13


def offsets():
    steps = range(-2, 3)
    return [
        (i, j, k)
        for i in steps
        for j in steps
        for k in steps
        if 0 < i * i + j * j + k * k <= 4
    ]


@functools.cache
def tables():
    rows = np.zeros(PAIRS, np.int32)
    column = np.zeros(2 * PAIRS, np.int32)
    site = np.zeros(2 * PAIRS, np.int32)
    domain = np.zeros(PAIRS, np.int32)
    slot = np.zeros(PAIRS, np.int32)
    shift = np.zeros((8, PAIRS), np.float32)
    for own in range(32):
        cell, inner = divmod(own, 8)
        at = (2 + 2 * (cell // 2) + inner // 4, 2 + inner // 2 % 2, 2 + 2 * (cell % 2) + inner % 2)
        for number, step in enumerate(offsets()):
            pair = own * 32 + number
            x, y, z = (u + v for u, v in zip(at, step))
            near_site = x % 2 * 4 + y % 2 * 2 + z % 2
            cx, cy, cz = x // 2, y // 2, z // 2
            rows[pair] = ((cx * 3 + cy) * 4 + cz) * 8 + near_site
            toward_x = -1 if cx == 0 else int(cx == 3)
            toward_z = -1 if cz == 0 else int(cz == 3)
            domain[pair] = (toward_x + 1) * 9 + cy * 3 + toward_z + 1
            near_cell = (cx - 1 - 2 * toward_x) * 2 + (cz - 1 - 2 * toward_z)
            slot[pair] = near_cell * 8 + near_site
            column[pair] = domain[pair] * 8 + near_cell
            column[PAIRS + pair] = HOME * 8 + cell
            site[pair] = near_site
            site[PAIRS + pair] = inner
            for axis in range(3):
                shift[axis, pair] = CELL_SIDE * ((x, y, z)[axis] // 2 - at[axis] // 2)
    pair = np.arange(PAIRS)
    own = pair // 32
    lane = np.arange(128)
    gather = rows[:, None] == np.arange(384)[None]
    from_domain = (domain[None] == np.arange(32)[:, None])
    pick = np.concatenate(
        [
            lane[:, None] % 32 == slot[None],
            lane[:, None] % 32 == own[None],
        ],
        axis=0,
    )
    scatter = np.arange(216)[:, None] == column[None]
    sites = np.arange(8)[:, None] == site[None]
    spread = np.zeros((128, 384), np.float32)
    for m in range(9):
        spread[8 + m, m:128:16] = 1.0
        spread[40 + m, 128 + m : 256 : 16] = 1.0
    spread[17, 256:] = 1.0
    spread[49, 256:] = 1.0
    return dict(
        gather=gather.astype(jnp.bfloat16),
        scatter=scatter.astype(jnp.bfloat16),
        pick=pick.astype(jnp.bfloat16),
        from_domain=from_domain.astype(np.float32),
        sites=sites.astype(np.float32),
        shift=shift,
        listed=rows.reshape(32, 32).astype(np.int32),
        spread=spread.astype(jnp.bfloat16),
    )


def mul(a, b):
    return lax.dot_general(a, b, (((1,), (0,)), ((), ())), preferred_element_type=F32)


def mul_t(a, b):
    return lax.dot_general(a, b, (((1,), (1,)), ((), ())), preferred_element_type=F32)


def split(a):
    high = a.astype(BF16)
    return high, (a - high.astype(F32)).astype(BF16)


def split3(a):
    high = a.astype(BF16)
    rest = a - high.astype(F32)
    mid = rest.astype(BF16)
    return high, mid, (rest - mid.astype(F32)).astype(BF16)


def iota(shape, axis):
    return lax.broadcasted_iota(jnp.int32, shape, axis)


def halves(a):
    return a[:, :CHANNELS] + a[:, CHANNELS:]


def beside(*parts):
    return jnp.concatenate(parts, axis=1)


def above(*parts):
    return jnp.concatenate(parts, axis=0)


def project(rows, weight_high, weight_low):
    high, low = split(rows)
    stacked = above(
        beside(weight_high, weight_low), beside(weight_high, jnp.zeros_like(weight_low))
    )
    return halves(mul(beside(high, low), stacked))


def position_row(positions):
    repeat = (iota((8, 128), 0) == iota((8, 128), 1) % 8).astype(F32).astype(BF16)
    spread = sum(mul(part, repeat) for part in split3(positions))
    own = iota((12, 128), 1) // 8 == iota((12, 128), 0)
    return jnp.sum(jnp.where(own, spread, 0.0), axis=0, keepdims=True)


def by_component(rows):
    lanes = iota(rows.shape, 1) // 32
    return above(*[jnp.where(lanes == axis, rows, 0.0) for axis in range(3)])


def listed_pairs(centers, counts, neighbours, listed):
    place = iota((32, 32), 1)
    names = jnp.where(place < counts, centers, 32) == iota((32, 32), 0)
    names = names.astype(F32)
    occupied = jnp.sum(names, axis=1, keepdims=True)
    name_bits = names.astype(BF16)
    entries = neighbours.astype(F32)
    coarse = jnp.floor(entries * (1.0 / 32.0))
    fine = entries - 32.0 * coarse
    by_slot = 32.0 * mul(name_bits, coarse.astype(BF16)) + mul(name_bits, fine.astype(BF16))
    wanted = listed.astype(F32)
    found = jnp.zeros((32, 32), F32)
    for entry in range(32):
        found = jnp.where(by_slot[:, entry : entry + 1] == wanted, 1.0, found)
    found = found * occupied
    spread_out = (iota((32, PAIRS), 1) % 32 == iota((32, PAIRS), 0)).astype(F32).astype(BF16)
    wide = mul(found.astype(BF16), spread_out)
    own = iota((32, PAIRS), 1) // 32 == iota((32, PAIRS), 0)
    return jnp.sum(jnp.where(own, wide, 0.0), axis=0, keepdims=True), occupied


def geometry(displace, live):
    dx = jnp.where(live > 0.0, displace[0:1], 6.0)
    dy = jnp.where(live > 0.0, displace[1:2], 0.0)
    dz = jnp.where(live > 0.0, displace[2:3], 0.0)
    length = jnp.sqrt(dx * dx + dy * dy + dz * dz)
    inverse = 1.0 / length
    ratio = length * (1.0 / CUTOFF)
    square = ratio * ratio
    fourth = square * square
    inside = ratio < 1.0
    weight = 1.0 + fourth * square * (-28.0 + ratio * (48.0 - 21.0 * ratio))
    weight = jnp.where(inside, weight, 0.0) * live
    gap = 1.0 - ratio
    slope = jnp.where(inside, (-168.0 / CUTOFF) * fourth * ratio * gap * gap, 0.0) * live
    frequency = (iota((8, PAIRS), 0) + 1).astype(F32) * math.pi
    phase = frequency * ratio
    scale = math.sqrt(2.0 / CUTOFF)
    basis = scale * jnp.sin(phase) * inverse
    basis_slope = (scale / CUTOFF * frequency * jnp.cos(phase) - basis) * inverse
    ex, ey, ez = dx * inverse, dy * inverse, dz * inverse
    three, fifteen, five = math.sqrt(3.0), math.sqrt(15.0), math.sqrt(5.0)
    angular = above(
        jnp.ones_like(ex),
        three * ex,
        three * ey,
        three * ez,
        fifteen * ex * ey,
        fifteen * ey * ez,
        0.5 * five * (3.0 * ez * ez - 1.0),
        fifteen * ex * ez,
        0.5 * fifteen * (ex * ex - ey * ey),
    )
    return dict(
        d=(dx, dy, dz), e=(ex, ey, ez), inverse=inverse, weight=weight, slope=slope,
        basis=basis, basis_slope=basis_slope, angular=angular,
    )


def pair_gradient(geo, grad_basis, grad_weight, grad_angular):
    ex, ey, ez = geo["e"]
    three, fifteen, five = math.sqrt(3.0), math.sqrt(15.0), math.sqrt(5.0)
    g = [grad_angular[m : m + 1] for m in range(9)]
    radial = grad_weight * geo["slope"] + jnp.sum(
        grad_basis * geo["basis_slope"], axis=0, keepdims=True
    )
    ux = three * g[1] + fifteen * (g[4] * ey + g[7] * ez + g[8] * ex)
    uy = three * g[2] + fifteen * (g[4] * ex + g[5] * ez - g[8] * ey)
    uz = three * g[3] + fifteen * (g[5] * ey + g[7] * ex) + 3.0 * five * g[6] * ez
    along = radial - geo["inverse"] * (ux * ex + uy * ey + uz * ez)
    return tuple(along * e + geo["inverse"] * u for e, u in zip((ex, ey, ez), (ux, uy, uz)))


def parcels(d, grad, sites, scatter):
    virial = [-0.5 * a * b for a in d for b in grad]
    near = [-g for g in grad] + virial
    home = list(grad) + virial
    near_sites, home_sites = sites[:, :PAIRS], sites[:, PAIRS:]
    zero = jnp.zeros((32, 2 * PAIRS), F32)
    stacked = above(
        beside(
            above(*[near_sites * part for part in near]),
            above(*[home_sites * part for part in home]),
        ),
        zero,
    )
    high, low = split(stacked)
    return mul_t(scatter, high) + mul_t(scatter, low)


def interactions(
    geo, near_rows, own_proj, pull_rows, gather, spread, basis_weight, paths, weights, own_rows
):
    (value_high, value_low, latent_high, latent_low, latent_t_high, latent_t_low,
     value_t_high, value_t_low) = weights
    stack = above(geo["basis"], geo["angular"], geo["weight"], jnp.zeros((14, PAIRS), F32))
    high = stack.astype(BF16).astype(F32)
    stack = above(high, stack - high, jnp.zeros((64, PAIRS), F32))
    scalars = jnp.transpose(stack).astype(BF16)
    basis_high, basis_low = split(basis_weight)
    near_high, near_low = split(near_rows)
    blank = jnp.zeros((24, CHANNELS), BF16)
    basis_rows = above(
        beside(basis_high, basis_low),
        beside(blank, blank),
        beside(basis_high, jnp.zeros_like(basis_low)),
        beside(blank, blank),
        jnp.zeros((64, 256), BF16),
    )
    table = above(beside(near_high, near_low), basis_rows)
    same_center = iota((256, 128), 0) // 32 == iota((256, 128), 1) // 16
    same_center_t = iota((128, 256), 1) // 32 == iota((128, 256), 0) // 16
    readout = above(
        beside(basis_weight, jnp.zeros((8, CHANNELS), F32)),
        beside(jnp.zeros((8, CHANNELS), F32), jnp.ones((8, CHANNELS), F32)),
    )
    readout_high, readout_low = split(readout)
    angular = above(geo["angular"], jnp.zeros((7, PAIRS), F32))
    sums, grad_scalars, grad_angulars = [], [], []
    for block in range(4):
        at = slice(block * 256, block * 256 + 256)
        rows = scalars[at]
        wide = mul(rows, spread)
        y_t_high = jnp.where(same_center, wide[:, :128], 0.0).astype(BF16)
        y_t_low = jnp.where(same_center, wide[:, 128:256], 0.0).astype(BF16)
        y_t = beside(y_t_high, y_t_low)
        y = jnp.where(same_center_t, above(*[angular[:, at]] * 8), 0.0)
        y_high, y_low = split(y)
        u = wide[:, 256:]
        h = halves(mul(beside(gather[at], rows), table)) + own_rows(own_proj, block)
        gate = jax.nn.sigmoid(h)
        silu = h * gate
        latent = u * silu
        l_high, l_low = split(latent)
        mixed = mul(beside(l_high, l_low), above(value_high, value_high)) + mul(l_high, value_low)
        value, env = mixed[:, :128], mixed[:, 128:]
        env_high, env_low = split(env)
        gamma = halves(mul(y_high, beside(env_high, env_low))) + mul(y_low, env_high)
        path = paths * gamma
        path_high, path_low = split(path)
        stacked = above(beside(path_high, path_low), beside(path_high, jnp.zeros_like(path_low)))
        inner = halves(mul(y_t, stacked))
        scalar = value * inner
        s_high, s_low = split(scalar)
        q = halves(mul(beside(l_high, s_high), beside(latent_high, latent_low)))
        q = q + mul(beside(l_low, s_low), latent_high)
        q_gate = jax.nn.sigmoid(q)
        update = q * q_gate
        sums.append(jnp.sum((latent + u * update).reshape(8, 32, CHANNELS), axis=1))
        pull = own_rows(pull_rows, block)
        grad_q = u * pull * (q_gate * (1.0 + q - update))
        g_high, g_low = split(grad_q)
        grad_joined = mul(beside(g_high, g_low), above(latent_t_high, latent_t_high))
        grad_joined = grad_joined + mul(g_high, latent_t_low)
        grad_latent = pull + grad_joined[:, :128]
        grad_scalar = grad_joined[:, 128:]
        grad_value = grad_scalar * inner
        grad_inner = grad_scalar * value
        i_high, i_low = split(grad_inner)
        grad_path = halves(mul(y_high, beside(i_high, i_low))) + mul(y_low, i_high)
        grad_gamma = paths * grad_path
        c_high, c_low = split(grad_gamma)
        stacked = above(beside(c_high, c_low), beside(c_high, jnp.zeros_like(c_low)))
        grad_env = halves(mul(y_t, stacked))
        v_high, v_low = split(grad_value)
        e_high, e_low = split(grad_env)
        grad_latent = grad_latent + halves(
            mul(beside(v_high, e_high), beside(value_t_high, value_t_low))
        ) + mul(beside(v_low, e_low), value_t_high)
        grad_h = grad_latent * u * (gate * (1.0 + h - silu))
        grad_u = pull * update + grad_latent * silu
        h_high, h_low = split(grad_h)
        u_high, u_low = split(grad_u)
        both = beside(h_high, u_high)
        grad_scalars.append(
            mul_t(readout_high, both)
            + mul_t(readout_high, beside(h_low, u_low))
            + mul_t(readout_low, both)
        )
        left_high, left_low = beside(path_high, c_high), beside(path_low, c_low)
        both = beside(i_high, env_high)
        cross = mul_t(left_high, both) + mul_t(left_high, beside(i_low, env_low))
        cross = cross + mul_t(left_low, both)
        cross = jnp.where(same_center_t, cross, 0.0)
        total = cross[0:16]
        for t in range(1, 8):
            total = total + cross[16 * t : 16 * t + 16]
        grad_angulars.append(total)
    return sums, beside(*grad_scalars), beside(*grad_angulars)


def path_rows(path_weight, scale):
    row = iota((128, CHANNELS), 0) % 16
    first, second, third = (path_weight[i : i + 1] for i in range(3))
    rows = jnp.where(row == 0, first, jnp.where(row < 4, second, third))
    return jnp.where(row < 9, rows, 0.0) * scale


def pull_of(occupied, species, scale, out_weight):
    return occupied * scale * out_weight * (ROOT_HALF / math.sqrt(32.0))


def of_kind(species, table):
    result = jnp.zeros(species.shape, F32)
    for kind in range(5):
        result = jnp.where(species == kind, table(kind), result)
    return result


def column_of(cells):
    rows = above(*[jnp.broadcast_to(cells[i : i + 1], (8, 8)) for i in range(4)])
    own = iota((32, 8), 0) % 8 == iota((32, 8), 1)
    return jnp.sum(jnp.where(own, rows, 0), axis=1, keepdims=True)


def row_of(column):
    eye = iota((8, 8), 0) == iota((8, 8), 1)
    return jnp.sum(jnp.where(eye, column, 0.0), axis=0, keepdims=True)


def kernel(
    shape,
    positions_ref, species_ref, centers_ref, neighbours_ref, counts_ref, scale_ref, shift_ref,
    listed_ref, cell_shift_ref,
    features_hbm, center_hbm, near_hbm, basis_hbm, path_hbm, value_hbm, latent_hbm, out_hbm,
    gather_hbm, scatter_hbm, pick_hbm, domain_hbm, sites_hbm, spread_hbm,
    energy_ref, forces_ref, virial_ref,
    frame, places, sent_place, returns, outgoing,
    center_w, near_w, basis_w, path_w, value_w, latent_w, out_w,
    gather_v, scatter_v, pick_v, domain_v, sites_v, spread_v, proj_v, pull_v,
    local_sem, send_sem, recv_sem,
):
    me = tuple(lax.axis_index(axis) for axis in ("gx", "gy", "gz"))

    def device(direction):
        return tuple(
            lax.rem(i + step + size, size) for i, step, size in zip(me, direction, shape)
        )

    others = [(i, d) for i, d in enumerate(DIRECTIONS) if i != HOME]
    barrier = pltpu.get_barrier_semaphore()
    for _, direction in others:
        pl.semaphore_signal(barrier, inc=1, device_id=device(direction), device_id_type=MESH)

    own_frame = frame.at[pl.ds(1, 2), pl.ds(1, 1), pl.ds(1, 2)]
    fetches = [(features_hbm, own_frame)] + list(
        zip(
            (center_hbm, near_hbm, basis_hbm, path_hbm, value_hbm, latent_hbm, out_hbm,
             gather_hbm, scatter_hbm, pick_hbm, domain_hbm, sites_hbm, spread_hbm),
            (center_w, near_w, basis_w, path_w, value_w, latent_w, out_w,
             gather_v, scatter_v, pick_v, domain_v, sites_v, spread_v),
        )
    )
    fetches = [
        pltpu.make_async_copy(src, dst, local_sem.at[i]) for i, (src, dst) in enumerate(fetches)
    ]
    for copy in fetches:
        copy.start()

    sent_place[...] = jnp.broadcast_to(
        position_row(positions_ref[...].reshape(12, 8)), (8, 128)
    )
    pl.semaphore_wait(barrier, 26)

    def span(step):
        return {1: (slice(1, 2), slice(0, 1)), -1: (slice(0, 1), slice(3, 4)), 0: (slice(0, 2), slice(1, 3))}[step]

    sends = []
    for index, (a, b, c) in others:
        (from_x, to_x), (from_z, to_z) = span(a), span(c)
        to_y = 1 - b
        sends.append(
            pltpu.make_async_remote_copy(
                src_ref=features_hbm.at[from_x, slice(0, 1), from_z],
                dst_ref=frame.at[to_x, slice(to_y, to_y + 1), to_z],
                send_sem=send_sem.at[index],
                recv_sem=recv_sem.at[index],
                device_id=device((a, b, c)),
                device_id_type=MESH,
            )
        )
        sends.append(
            pltpu.make_async_remote_copy(
                src_ref=sent_place,
                dst_ref=places.at[26 - index],
                send_sem=send_sem.at[27 + index],
                recv_sem=recv_sem.at[27 + index],
                device_id=device((a, b, c)),
                device_id_type=MESH,
            )
        )
    for copy in sends:
        copy.start()

    live, occupied = listed_pairs(
        centers_ref[...], counts_ref[...], neighbours_ref[...], listed_ref[...]
    )
    for copy in fetches:
        copy.wait()
    species = column_of(species_ref[...].reshape(4, 8))
    scale = of_kind(species, lambda kind: scale_ref[kind])
    shift = of_kind(species, lambda kind: shift_ref[kind])
    pull_v[...] = occupied * scale * out_w[...] * (ROOT_HALF / math.sqrt(32.0))
    own = frame[1:3, 1:2, 1:3].reshape(32, CHANNELS)
    proj_v[...] = project(own, *split(center_w[...]))
    own_place = sum(
        mul(part, pick_v[128:256]) for part in split3(by_component(sent_place[0:1]))
    )
    base = cell_shift_ref[0:3] - own_place
    value, latent = value_w[...], latent_w[...]
    weights = (
        split(value) + split(latent) + split(jnp.transpose(latent)) + split(jnp.transpose(value))
    )
    near_high, near_low = split(near_w[...])
    paths = path_rows(path_w[...], 1.0 / math.sqrt(32.0))

    for copy in sends:
        copy.wait_recv()

    near_rows = project(frame[...].reshape(384, CHANNELS), near_high, near_low)
    place_rows = above(
        jnp.concatenate([places[i, 0:1] for i in range(HOME)], axis=0),
        sent_place[0:1],
        jnp.concatenate([places[i, 0:1] for i in range(HOME + 1, 27)], axis=0),
        jnp.zeros((5, 128), F32),
    )
    gathered = sum(mul(part, pick_v[0:128]) for part in split3(by_component(place_rows)))
    chosen = above(
        *[
            jnp.sum(gathered[32 * i : 32 * i + 32] * domain_v[...], axis=0, keepdims=True)
            for i in range(3)
        ]
    )
    geo = geometry(chosen + base, live)

    def own_rows(ref, block):
        return above(
            *[
                jnp.broadcast_to(ref[pl.ds(block * 8 + t, 1), :], (32, CHANNELS))
                for t in range(8)
            ]
        )

    sums, grad_scalars, grad_angular = interactions(
        geo, near_rows, proj_v, pull_v, gather_v[...], spread_v[...], basis_w[...], paths,
        weights, own_rows,
    )
    grad = pair_gradient(geo, grad_scalars[0:8], grad_scalars[8:9], grad_angular)
    outgoing[...] = halves_of(parcels(geo["d"], grad, sites_v[...], scatter_v[...]))

    backs = []
    for index, direction in others:
        backs.append(
            pltpu.make_async_remote_copy(
                src_ref=outgoing.at[index],
                dst_ref=returns.at[26 - index],
                send_sem=send_sem.at[54 + index],
                recv_sem=recv_sem.at[54 + index],
                device_id=device(direction),
                device_id_type=MESH,
            )
        )
    for copy in backs:
        copy.start()

    for block in range(4):
        at = slice(block * 8, block * 8 + 8)
        energy = jnp.sum(sums[block] * out_w[...], axis=1, keepdims=True)
        energy = energy * (ROOT_HALF / math.sqrt(32.0))
        energy = occupied[at] * (scale[at] * energy + shift[at])
        energy_ref[block // 2, 0, block % 2 : block % 2 + 1, :] = row_of(energy)

    for copy in sends:
        copy.wait_send()
    for copy in backs:
        copy.wait_recv()
    total = outgoing[HOME]
    for index, _ in others:
        total = total + returns[index]
    for component in range(12):
        ref, where = (forces_ref, component) if component < 3 else (virial_ref, component - 3)
        piece = total[0:4, component * 8 : component * 8 + 8]
        for cx in range(2):
            ref[where, cx, 0] = piece[2 * cx : 2 * cx + 2]
    for copy in backs:
        copy.wait_send()


def halves_of(rows):
    return rows.reshape(27, 8, CHANNELS)


def local(shape, *arguments):
    (positions, features, species, centers, neighbours, counts, species_scale, species_shift,
     center_weight, near_weight, basis_weight, path_weight, value_weight, latent_weight,
     out_weight) = arguments
    fixed = {name: jnp.asarray(value) for name, value in tables().items()}
    vmem = pl.BlockSpec(memory_space=pltpu.VMEM)
    smem = pl.BlockSpec(memory_space=pltpu.SMEM)
    any_ = pl.BlockSpec(memory_space=pl.ANY)
    hbm = pl.BlockSpec(memory_space=pltpu.HBM)
    return pl.pallas_call(
        functools.partial(kernel, shape),
        out_shape=(
            jax.ShapeDtypeStruct((2, 1, 2, 8), F32),
            jax.ShapeDtypeStruct((3, 2, 1, 2, 8), F32),
            jax.ShapeDtypeStruct((9, 2, 1, 2, 8), F32),
        ),
        in_specs=[vmem] * 5 + [smem] * 2 + [vmem] * 2 + [any_] * 14,
        out_specs=(vmem,) * 3,
        scratch_shapes=[
            pltpu.VMEM((4, 3, 4, 8, CHANNELS), F32),
            pltpu.VMEM((27, 8, 128), F32),
            pltpu.VMEM((8, 128), F32),
            pltpu.VMEM((27, 8, 128), F32),
            pltpu.VMEM((27, 8, 128), F32),
            pltpu.VMEM((128, 128), F32),
            pltpu.VMEM((128, 128), F32),
            pltpu.VMEM((8, 128), F32),
            pltpu.VMEM((3, 128), F32),
            pltpu.VMEM((128, 256), F32),
            pltpu.VMEM((256, 128), F32),
            pltpu.VMEM((1, 128), F32),
            pltpu.VMEM((1024, 384), BF16),
            pltpu.VMEM((216, 2048), BF16),
            pltpu.VMEM((256, 1024), BF16),
            pltpu.VMEM((32, 1024), F32),
            pltpu.VMEM((8, 2048), F32),
            pltpu.VMEM((128, 384), BF16),
            pltpu.VMEM((32, 128), F32),
            pltpu.VMEM((32, 128), F32),
            pltpu.SemaphoreType.DMA((14,)),
            pltpu.SemaphoreType.DMA((81,)),
            pltpu.SemaphoreType.DMA((81,)),
        ],
        compiler_params=pltpu.CompilerParams(
            collective_id=0, has_side_effects=True, vmem_limit_bytes=56 * 1024 * 1024
        ),
        name="allegro",
    )(
        positions, species, centers.reshape(1, 32), neighbours, counts.reshape(1, 1),
        species_scale, species_shift, fixed["listed"], fixed["shift"],
        features, center_weight, near_weight, basis_weight, path_weight, value_weight,
        latent_weight, out_weight.reshape(1, 128), fixed["gather"], fixed["scatter"],
        fixed["pick"], fixed["from_domain"], fixed["sites"], fixed["spread"],
    )


def solution(mesh):
    placed = (
        P(None, "gx", "gy", "gz", None),
        P("gx", "gy", "gz", None, None),
        P("gx", "gy", "gz", None),
        P(("gx", "gy", "gz")),
        P(("gx", "gy", "gz"), None),
        P(("gx", "gy", "gz")),
    ) + (P(),) * 9
    shape = tuple(mesh.shape[axis] for axis in ("gx", "gy", "gz"))
    return jax.shard_map(
        functools.partial(local, shape),
        mesh=mesh,
        in_specs=placed,
        out_specs=(
            P("gx", "gy", "gz", None),
            P(None, "gx", "gy", "gz", None),
            P(None, "gx", "gy", "gz", None),
        ),
        check_vma=False,
    )
```

```python
import functools
import math

import jax
import jax.numpy as jnp
import numpy as np
from jax import lax
from jax.experimental import pallas as pl
from jax.experimental.pallas import tpu as pltpu
from jax.sharding import PartitionSpec as P

MESH = pl.DeviceIdType.MESH
F32 = jnp.float32
BF16 = jnp.bfloat16
CUTOFF = 5.0
CELL_SIDE = 4.6
ROOT_HALF = 0.7071067811865476
CHANNELS = 128
PAIRS = 1024
DIRECTIONS = [(a, b, c) for a in (-1, 0, 1) for b in (-1, 0, 1) for c in (-1, 0, 1)]
HOME = 13
CHUNK = 1024


def offsets():
    steps = range(-2, 3)
    return [
        (i, j, k)
        for i in steps
        for j in steps
        for k in steps
        if 0 < i * i + j * j + k * k <= 4
    ]


@functools.cache
def pairs():
    result = []
    for own in range(32):
        cell, inner = divmod(own, 8)
        at = (2 + 2 * (cell // 2) + inner // 4, 2 + inner // 2 % 2, 2 + 2 * (cell % 2) + inner % 2)
        for step in offsets():
            place = tuple(u + v for u, v in zip(at, step))
            site = place[0] % 2 * 4 + place[1] % 2 * 2 + place[2] % 2
            cx, cy, cz = (u // 2 for u in place)
            row = ((cx * 3 + cy) * 4 + cz) * 8 + site
            toward_x = -1 if cx == 0 else int(cx == 3)
            toward_z = -1 if cz == 0 else int(cz == 3)
            direction = (toward_x + 1) * 9 + cy * 3 + toward_z + 1
            near_cell = (cx - 1 - 2 * toward_x) * 2 + (cz - 1 - 2 * toward_z)
            shift = [CELL_SIDE * (u // 2 - v // 2) for u, v in zip(place, at)]
            result.append((own, row, direction, near_cell * 8 + site, shift))
    return result


@functools.cache
def wanted():
    slots = [sorted({p[3] for p in pairs() if p[2] == i}) for i in range(27)]
    slots[HOME] = list(range(32))
    order = [HOME] + sorted(
        (i for i in range(27) if i != HOME),
        key=lambda i: (sum(map(bool, DIRECTIONS[i])), i),
    )
    starts, row = {}, 0
    for i in order:
        starts[i] = row
        row += len(slots[i])
    return slots, starts, order


@functools.cache
def tables():
    slots, starts, _ = wanted()
    near = np.array([starts[p[2]] + slots[p[2]].index(p[3]) for p in pairs()])
    own = np.array([p[0] for p in pairs()])
    direction = np.array([p[2] for p in pairs()])
    slot = np.array([p[3] for p in pairs()])
    lane = np.arange(128)
    shift = np.zeros((8, PAIRS), np.float32)
    shift[:3] = np.array([p[4] for p in pairs()]).T
    column = np.concatenate([direction * 4 + slot // 8, HOME * 4 + own // 8])
    site = np.concatenate([slot % 8, own % 8])
    return dict(
        gather=(near[:, None] == np.arange(256)[None]).astype(jnp.bfloat16),
        scatter=(np.arange(112)[:, None] == column[None]).astype(jnp.bfloat16),
        pick=np.concatenate(
            [lane[:, None] % 32 == slot[None], lane[:, None] % 32 == own[None]], axis=0
        ).astype(jnp.bfloat16),
        from_domain=(direction[None] == np.arange(32)[:, None]).astype(np.float32),
        sites=(np.arange(8)[:, None] == site[None]).astype(np.float32),
        shift=shift,
        listed=np.array([p[1] for p in pairs()]).reshape(32, 32).astype(np.int32),
    )


def mul(a, b):
    return lax.dot_general(a, b, (((1,), (0,)), ((), ())), preferred_element_type=F32)


def mul_t(a, b):
    return lax.dot_general(a, b, (((1,), (1,)), ((), ())), preferred_element_type=F32)


def split(a):
    high = a.astype(BF16)
    return high, (a - high.astype(F32)).astype(BF16)


def split3(a):
    high = a.astype(BF16)
    rest = a - high.astype(F32)
    mid = rest.astype(BF16)
    return high, mid, (rest - mid.astype(F32)).astype(BF16)


def iota(shape, axis):
    return lax.broadcasted_iota(jnp.int32, shape, axis)


def halves(a):
    return a[:, :CHANNELS] + a[:, CHANNELS:]


def beside(*parts):
    return jnp.concatenate(parts, axis=1)


def above(*parts):
    return jnp.concatenate(parts, axis=0)


def stack_of(high, low):
    return above(beside(high, low), beside(high, jnp.zeros_like(low)))


def project(rows, weight):
    return halves(mul(beside(*split(rows)), stack_of(*split(weight))))


def position_row(positions):
    repeat = (iota((8, 128), 0) == iota((8, 128), 1) % 8).astype(F32).astype(BF16)
    spread = sum(mul(part, repeat) for part in split3(positions))
    own = iota((12, 128), 1) // 8 == iota((12, 128), 0)
    return jnp.sum(jnp.where(own, spread, 0.0), axis=0, keepdims=True)


def by_component(rows):
    lanes = iota(rows.shape, 1) // 32
    return above(*[jnp.where(lanes == axis, rows, 0.0) for axis in range(3)])


def listed_pairs(centers, neighbours, listed):
    names = (centers == iota((32, 32), 0)).astype(F32)
    occupied = jnp.sum(names, axis=1, keepdims=True)
    name_bits = names.astype(BF16)
    entries = neighbours.astype(F32)
    coarse = jnp.floor(entries * (1.0 / 32.0))
    fine = entries - 32.0 * coarse
    by_slot = 32.0 * mul(name_bits, coarse.astype(BF16)) + mul(name_bits, fine.astype(BF16))
    wanted = listed.astype(F32)
    found = jnp.zeros((32, 32), F32)
    for entry in range(32):
        found = jnp.where(by_slot[:, entry : entry + 1] == wanted, 1.0, found)
    found = found * occupied
    spread_out = (iota((32, PAIRS), 1) % 32 == iota((32, PAIRS), 0)).astype(F32).astype(BF16)
    wide = mul(found.astype(BF16), spread_out)
    own = iota((32, PAIRS), 1) // 32 == iota((32, PAIRS), 0)
    return jnp.sum(jnp.where(own, wide, 0.0), axis=0, keepdims=True), occupied


def sine_cosine(ratio):
    angle = (ratio - 0.5) * math.pi
    square = angle * angle
    sine, cosine = jnp.zeros_like(ratio), jnp.zeros_like(ratio)
    for k in range(6, -1, -1):
        sign = (-1.0) ** k
        cosine = cosine * square + sign / math.factorial(2 * k)
        if k < 6:
            sine = sine * square + sign / math.factorial(2 * k + 1)
    return cosine, -sine * angle


def multiples(sine, cosine):
    s, c = {1: sine}, {1: cosine}
    for m in range(2, 9):
        if m % 2 == 0:
            h = m // 2
            s[m] = 2.0 * s[h] * c[h]
            c[m] = 1.0 - 2.0 * s[h] * s[h]
        else:
            a, b = m // 2, m - m // 2
            s[m] = s[a] * c[b] + c[a] * s[b]
            c[m] = c[a] * c[b] - s[a] * s[b]
    order = range(1, 9)
    return above(*[s[m] for m in order]), above(*[c[m] for m in order])


def geometry(displace, live):
    dx = jnp.where(live > 0.0, displace[0:1], 6.0)
    dy = jnp.where(live > 0.0, displace[1:2], 0.0)
    dz = jnp.where(live > 0.0, displace[2:3], 0.0)
    length = jnp.sqrt(dx * dx + dy * dy + dz * dz)
    inverse = 1.0 / length
    ratio = length * (1.0 / CUTOFF)
    square = ratio * ratio
    fourth = square * square
    inside = ratio < 1.0
    weight = 1.0 + fourth * square * (-28.0 + ratio * (48.0 - 21.0 * ratio))
    weight = jnp.where(inside, weight, 0.0) * live
    gap = 1.0 - ratio
    slope = jnp.where(inside, (-168.0 / CUTOFF) * fourth * ratio * gap * gap, 0.0) * live
    frequency = (iota((8, PAIRS), 0) + 1).astype(F32) * math.pi
    sines, cosines = multiples(*sine_cosine(jnp.minimum(ratio, 1.0)))
    scale = math.sqrt(2.0 / CUTOFF)
    basis = scale * sines * inverse
    basis_slope = (scale / CUTOFF * frequency * cosines - basis) * inverse
    ex, ey, ez = dx * inverse, dy * inverse, dz * inverse
    three, fifteen, five = math.sqrt(3.0), math.sqrt(15.0), math.sqrt(5.0)
    angular = above(
        three * ex,
        three * ey,
        three * ez,
        fifteen * ex * ey,
        fifteen * ey * ez,
        0.5 * five * (3.0 * ez * ez - 1.0),
        fifteen * ex * ez,
        0.5 * fifteen * (ex * ex - ey * ey),
    )
    return dict(
        d=(dx, dy, dz), e=(ex, ey, ez), inverse=inverse, weight=weight, slope=slope,
        basis=basis, basis_slope=basis_slope, angular=angular,
    )


def pair_gradient(geo, grad_basis, grad_weight, grad_angular):
    ex, ey, ez = geo["e"]
    three, fifteen, five = math.sqrt(3.0), math.sqrt(15.0), math.sqrt(5.0)
    g = [None] + [grad_angular[m : m + 1] for m in range(8)]
    radial = grad_weight * geo["slope"] + jnp.sum(
        grad_basis * geo["basis_slope"], axis=0, keepdims=True
    )
    ux = three * g[1] + fifteen * (g[4] * ey + g[7] * ez + g[8] * ex)
    uy = three * g[2] + fifteen * (g[4] * ex + g[5] * ez - g[8] * ey)
    uz = three * g[3] + fifteen * (g[5] * ey + g[7] * ex) + 3.0 * five * g[6] * ez
    along = radial - geo["inverse"] * (ux * ex + uy * ey + uz * ez)
    return tuple(along * e + geo["inverse"] * u for e, u in zip((ex, ey, ez), (ux, uy, uz)))


def parcels(d, grad, sites, scatter):
    virial = [-0.5 * a * b for a in d for b in grad]
    near = [-g for g in grad] + virial
    home = list(grad) + virial
    near_sites, home_sites = sites[:, :PAIRS], sites[:, PAIRS:]
    stacked = beside(
        above(*[near_sites * part for part in near]),
        above(*[home_sites * part for part in home]),
    )
    high, low = split(stacked)
    zero = jnp.zeros((32, 2 * PAIRS), BF16)
    return halves(mul_t(scatter, above(high, zero, low, zero)))


def interactions(geo, near_rows, own_proj, pull_rows, gather, basis_weight, paths, weights, chunk):
    (value_high, value_low, latent_high, latent_low, latent_t_high, latent_t_low,
     value_t_high, value_t_low) = weights
    basis_high, basis_low = split(basis_weight)
    near_high, near_low = split(near_rows)
    table = above(
        beside(near_high, near_low),
        beside(basis_high, basis_low),
        beside(basis_high, jnp.zeros_like(basis_low)),
        jnp.zeros((32, 256), BF16),
    )
    readout = above(
        beside(basis_weight, jnp.zeros((8, CHANNELS), F32)),
        beside(jnp.zeros((8, CHANNELS), F32), jnp.ones((8, CHANNELS), F32)),
    )
    readout_high, readout_low = split(readout)
    value_both = above(value_high, value_high)
    latent_both = beside(latent_high, latent_low)
    latent_t_both = above(latent_t_high, latent_t_high)
    value_t_both = beside(value_t_high, value_t_low)
    of_center = [
        (iota((8, 256), 1) // 32 == t).astype(F32) for t in range(8)
    ]
    ones = (iota((8, 256), 1) // 32 == iota((8, 256), 0)).astype(F32)
    basis_top = geo["basis"].astype(BF16).astype(F32)
    basis_rest = geo["basis"] - basis_top
    lane = iota((256, 128), 1)
    sums, grad_scalars, grad_angulars = [], [], []
    per = chunk // 256
    spare = jnp.zeros((56, 256), BF16)

    def stacked_paths(high, low):
        return above(
            beside(high, low), spare, beside(high, jnp.zeros_like(low)), spare
        )

    for first in range(0, 4, per):
        blocks = range(first, first + per)
        ys, y_ts, us, lefts = [], [], [], []
        for block in blocks:
            at = slice(block * 256, block * 256 + 256)
            angular = geo["angular"][:, at]
            y = above(*[angular * of_center[t] for t in range(8)], ones)
            flat = jnp.transpose(
                above(
                    y,
                    jnp.zeros((8, 256), F32),
                    basis_top[:, at],
                    basis_rest[:, at],
                    jnp.broadcast_to(geo["weight"][:, at], (8, 256)),
                    jnp.zeros((24, 256), F32),
                )
            )
            ys.append(split(y))
            y_ts.append(beside(*split(jnp.where(lane < 72, flat, 0.0))))
            us.append(jnp.broadcast_to(flat[:, 96:97], (256, 128)))
            radial = jnp.where((lane >= 80) & (lane < 96), flat, 0.0).astype(BF16)
            lefts.append(beside(gather[at, :128], gather[at, 128:] + radial))
        u = above(*us)
        h = halves(mul(above(*lefts), table)) + own_rows(own_proj, blocks)
        gate = jax.nn.sigmoid(h)
        silu = h * gate
        latent = u * silu
        l_high, l_low = split(latent)
        mixed = mul(beside(l_high, l_low), value_both) + mul(l_high, value_low)
        value, env = mixed[:, :128], mixed[:, 128:]
        env_high, env_low = split(env)
        inners, path_parts = [], []
        for k, block in enumerate(blocks):
            at = slice(k * 256, k * 256 + 256)
            y_high, y_low = ys[k]
            gamma = halves(mul(y_high, beside(env_high[at], env_low[at])))
            gamma = gamma + mul(y_low, env_high[at])
            parts = split(paths * gamma)
            path_parts.append(parts)
            inners.append(halves(mul(y_ts[k], stacked_paths(*parts))))
        inner = above(*inners)
        s_high, s_low = split(value * inner)
        q = halves(mul(beside(l_high, s_high), latent_both))
        q = q + mul(beside(l_low, s_low), latent_high)
        q_gate = jax.nn.sigmoid(q)
        update = q * q_gate
        sums.append(jnp.sum((latent + u * update).reshape(8 * per, 32, CHANNELS), axis=1))
        pull = own_rows(pull_rows, blocks)
        grad_q = u * pull * (q_gate * (1.0 + q - update))
        g_high, g_low = split(grad_q)
        grad_joined = mul(beside(g_high, g_low), latent_t_both) + mul(g_high, latent_t_low)
        grad_scalar = grad_joined[:, 128:]
        i_high, i_low = split(grad_scalar * value)
        v_high, v_low = split(grad_scalar * inner)
        grad_envs = []
        for k, block in enumerate(blocks):
            at = slice(k * 256, k * 256 + 256)
            y_high, y_low = ys[k]
            grad_path = halves(mul(y_high, beside(i_high[at], i_low[at])))
            grad_path = grad_path + mul(y_low, i_high[at])
            c_high, c_low = split(paths * grad_path)
            grad_envs.append(halves(mul(y_ts[k], stacked_paths(c_high, c_low))))
            path_high, path_low = path_parts[k]
            left_high = beside(path_high[:64], c_high[:64])
            left_low = beside(path_low[:64], c_low[:64])
            both = beside(i_high[at], env_high[at])
            cross = mul_t(above(left_high, left_low), both)
            cross = cross[:64] + cross[64:]
            cross = cross + mul_t(left_high, beside(i_low[at], env_low[at]))
            total = cross[0:8] * of_center[0]
            for t in range(1, 8):
                total = total + cross[8 * t : 8 * t + 8] * of_center[t]
            grad_angulars.append(total)
        e_high, e_low = split(above(*grad_envs))
        grad_latent = pull + grad_joined[:, :128]
        grad_latent = grad_latent + halves(mul(beside(v_high, e_high), value_t_both))
        grad_latent = grad_latent + mul(beside(v_low, e_low), value_t_high)
        grad_h = grad_latent * u * (gate * (1.0 + h - silu))
        grad_u = pull * update + grad_latent * silu
        h_high, h_low = split(grad_h)
        u_high, u_low = split(grad_u)
        both = mul_t(above(readout_high, readout_low), beside(h_high, u_high))
        grad_scalars.append(
            both[:16] + both[16:] + mul_t(readout_high, beside(h_low, u_low))
        )
    return above(*sums), beside(*grad_scalars), beside(*grad_angulars)


def own_rows(ref, blocks):
    return above(
        *[
            jnp.broadcast_to(ref[pl.ds(block * 8 + t, 1), :], (32, CHANNELS))
            for block in blocks
            for t in range(8)
        ]
    )


def path_rows(path_weight, scale):
    row = iota((72, CHANNELS), 0)
    first, second, third = (path_weight[i : i + 1] for i in range(3))
    return jnp.where(row >= 64, first, jnp.where(row % 8 < 3, second, third)) * scale


def of_kind(species, table):
    result = jnp.zeros(species.shape, F32)
    for kind in range(5):
        result = jnp.where(species == kind, table[0:1, kind : kind + 1], result)
    return result


def column_of(cells):
    rows = above(*[jnp.broadcast_to(cells[i : i + 1], (8, 8)) for i in range(4)])
    own = iota((32, 8), 0) % 8 == iota((32, 8), 1)
    return jnp.sum(jnp.where(own, rows, 0), axis=1, keepdims=True)


def kernel(
    shape,
    positions_hbm, features_hbm, near_hbm,
    species_hbm, centers_hbm, neighbours_hbm, scale_hbm, shift_hbm,
    center_hbm, basis_hbm, path_hbm, value_hbm, latent_hbm, out_hbm,
    listed_hbm, cell_shift_hbm, gather_hbm, scatter_hbm, pick_hbm, domain_hbm, sites_hbm,
    result_ref,
    positions_w, own_w, near_w,
    species_w, centers_w, neighbours_w, scale_w, shift_w,
    center_w, basis_w, path_w, value_w, latent_w, out_w,
    listed_v, cell_shift_v, gather_v, scatter_v, pick_v, domain_v, sites_v,
    mine, message, halo, few, places, returns, outgoing, proj_v, pull_v, ledger,
    local_sem, send_sem, recv_sem,
):
    me = tuple(lax.axis_index(axis) for axis in ("gx", "gy", "gz"))

    def device(direction):
        return tuple(
            lax.rem(i + step + size, size) for i, step, size in zip(me, direction, shape)
        )

    others = [(i, d) for i, d in enumerate(DIRECTIONS) if i != HOME]
    far_first = sorted(others, key=lambda item: -sum(map(abs, item[1])))
    barrier = pltpu.get_barrier_semaphore()
    for _, direction in far_first:
        pl.semaphore_signal(barrier, inc=1, device_id=device(direction), device_id_type=MESH)

    sources = (
        positions_hbm, features_hbm, near_hbm, species_hbm, centers_hbm, neighbours_hbm,
        scale_hbm, shift_hbm, center_hbm, basis_hbm, path_hbm, value_hbm, latent_hbm, out_hbm,
        listed_hbm, cell_shift_hbm, gather_hbm, scatter_hbm, pick_hbm, domain_hbm, sites_hbm,
    )
    targets = (
        positions_w, own_w, near_w, species_w, centers_w, neighbours_w,
        scale_w, shift_w, center_w, basis_w, path_w, value_w, latent_w, out_w,
        listed_v, cell_shift_v, gather_v, scatter_v, pick_v, domain_v, sites_v,
    )
    fetches = [
        pltpu.make_async_copy(src, dst, local_sem.at[i])
        for i, (src, dst) in enumerate(zip(sources, targets))
    ]
    for copy in fetches:
        copy.start()

    slots, starts, order = wanted()
    for copy in fetches[:3]:
        copy.wait()
    own = own_w[...].reshape(32, CHANNELS)
    mine[...] = project(own, near_w[...])
    place = position_row(positions_w[...].reshape(12, 8))
    places[...] = jnp.zeros_like(places)
    places[HOME : HOME + 1, :] = place
    for index, _ in others:
        taken = slots[26 - index]
        done = 0
        while done < len(taken):
            run = 1
            while done + run < len(taken) and taken[done + run] == taken[done] + run:
                run += 1
            message[index, done : done + run] = mine[taken[done] : taken[done] + run]
            done += run
        message[index, done : done + 1] = place
    pl.semaphore_wait(barrier, 26)

    for index, direction in far_first:
        rows = pl.ds(0, len(slots[26 - index]) + 1)
        pltpu.make_async_remote_copy(
            src_ref=message.at[index, rows],
            dst_ref=halo.at[26 - index, rows],
            send_sem=send_sem.at[0],
            recv_sem=recv_sem.at[0],
            device_id=device(direction),
            device_id_type=MESH,
        ).start()

    def settle(rows, semaphore):
        ref = ledger.at[pl.ds(0, rows)]
        pltpu.make_async_copy(ref, ref, semaphore).wait()

    sent_rows = sum(len(slots[i]) + 1 for i, _ in others)

    for copy in fetches[3:]:
        copy.wait()
    live, occupied = listed_pairs(centers_w[...], neighbours_w[...], listed_v[...])
    species = column_of(species_w[...].reshape(4, 8))
    scale = of_kind(species, scale_w[...])
    shift = of_kind(species, shift_w[...])
    pull_v[...] = occupied * scale * out_w[...] * (ROOT_HALF / math.sqrt(32.0))
    proj_v[...] = project(own, center_w[...])
    own_place = sum(mul(part, pick_v[128:256]) for part in split3(by_component(place)))
    base = cell_shift_v[0:3] - own_place[0:3]
    value, latent = value_w[...], latent_w[...]
    weights = (
        split(value) + split(latent) + split(jnp.transpose(latent)) + split(jnp.transpose(value))
    )
    paths = path_rows(path_w[...], 1.0 / math.sqrt(32.0))

    settle(sent_rows, recv_sem.at[0])

    for index, _ in others:
        count = len(slots[index])
        places[index : index + 1, :] = halo[index, count : count + 1]
        if count < 16:
            start = starts[index] - 160
            few[start : start + count, :] = halo[index, 0:count]
    near_rows = above(
        mine[...], *[halo[i, 0 : len(slots[i])] for i in order[1:7]], few[...]
    )
    gathered = sum(mul(part, pick_v[0:128]) for part in split3(by_component(places[...])))
    chosen = above(
        *[
            jnp.sum(gathered[32 * i : 32 * i + 32] * domain_v[...], axis=0, keepdims=True)
            for i in range(3)
        ]
    )
    geo = geometry(chosen + base, live)
    sums, grad_scalars, grad_angular = interactions(
        geo, near_rows, proj_v, pull_v, gather_v, basis_w[...], paths, weights, CHUNK
    )
    grad = pair_gradient(geo, grad_scalars[0:8], grad_scalars[8:9], grad_angular)
    owed = parcels(geo["d"], grad, sites_v[...], scatter_v[...])
    for index in range(27):
        outgoing[index, 0:4] = owed[4 * index : 4 * index + 4]

    rows = pl.ds(0, 4)
    for index, direction in far_first:
        pltpu.make_async_remote_copy(
            src_ref=outgoing.at[index, rows],
            dst_ref=returns.at[26 - index, rows],
            send_sem=send_sem.at[1],
            recv_sem=recv_sem.at[1],
            device_id=device(direction),
            device_id_type=MESH,
        ).start()

    energy = jnp.sum(sums * out_w[...], axis=1, keepdims=True) * (ROOT_HALF / math.sqrt(32.0))
    energy = occupied * (scale * energy + shift)
    at_lane = iota((32, 128), 1) == 96 + iota((32, 128), 0) % 8
    energies = jnp.sum(jnp.where(at_lane, energy, 0.0).reshape(4, 8, 128), axis=1)
    total = outgoing[HOME, 0:4] + energies
    settle(sent_rows, send_sem.at[0])
    settle(104, recv_sem.at[1])
    for index, _ in others:
        total = total + returns[index, 0:4]
    result_ref[0:4, :] = total
    result_ref[4:8, :] = jnp.zeros((4, 128), F32)
    settle(104, send_sem.at[1])


def finish(total_ref, energy_ref, forces_ref, virial_ref):
    total = total_ref[0:4, :]
    energy = total[:, 96:104]
    for cx in range(2):
        energy_ref[cx, 0] = energy[2 * cx : 2 * cx + 2]
    for component in range(3):
        piece = total[:, component * 8 : component * 8 + 8]
        for cx in range(2):
            forces_ref[component, cx, 0] = piece[2 * cx : 2 * cx + 2]
    rows = above(*[jnp.broadcast_to(total[i : i + 1], (8, 128)) for i in range(4)])
    rows = jnp.where(iota((32, 128), 1) % 8 == iota((32, 128), 0) % 8, rows, 0.0)
    fold = (iota((128, 128), 0) // 8 - 3 == iota((128, 128), 1)).astype(F32).astype(BF16)
    by_site = sum(mul(part, fold) for part in split3(rows))
    for cell in range(4):
        virial_ref[cell // 2, 0, cell % 2] = by_site[8 * cell : 8 * cell + 8, 0:9]


def local(shape, *arguments):
    (positions, features, species, centers, neighbours, _, species_scale, species_shift,
     center_weight, near_weight, basis_weight, path_weight, value_weight, latent_weight,
     out_weight) = arguments
    fixed = {name: jnp.asarray(value) for name, value in tables().items()}
    vmem = pl.BlockSpec(memory_space=pltpu.VMEM)
    operands = (
        positions, features, near_weight,
        species, centers.reshape(1, 32), neighbours, species_scale.reshape(1, 5),
        species_shift.reshape(1, 5), center_weight, basis_weight, path_weight, value_weight,
        latent_weight, out_weight.reshape(1, 128),
        fixed["listed"], fixed["shift"], fixed["gather"], fixed["scatter"], fixed["pick"],
        fixed["from_domain"], fixed["sites"],
    )
    total = pl.pallas_call(
        functools.partial(kernel, shape),
        out_shape=jax.ShapeDtypeStruct((8, 128), F32),
        in_specs=[pl.BlockSpec(memory_space=pl.ANY)] * len(operands),
        out_specs=vmem,
        scratch_shapes=[pltpu.VMEM(x.shape, x.dtype) for x in operands]
        + [
            pltpu.VMEM((32, CHANNELS), F32),
            pltpu.VMEM((27, 40, CHANNELS), F32),
            pltpu.VMEM((27, 40, CHANNELS), F32),
            pltpu.VMEM((48, CHANNELS), F32),
            pltpu.VMEM((32, 128), F32),
            pltpu.VMEM((27, 8, 128), F32),
            pltpu.VMEM((27, 8, 128), F32),
            pltpu.VMEM((32, CHANNELS), F32),
            pltpu.VMEM((32, CHANNELS), F32),
            pltpu.VMEM((208, 128), F32),
            pltpu.SemaphoreType.DMA((len(operands),)),
            pltpu.SemaphoreType.DMA((2,)),
            pltpu.SemaphoreType.DMA((2,)),
        ],
        compiler_params=pltpu.CompilerParams(
            collective_id=0, has_side_effects=True, vmem_limit_bytes=56 * 1024 * 1024
        ),
        name="allegro",
    )(*operands)
    energy, forces, virial = pl.pallas_call(
        finish,
        out_shape=(
            jax.ShapeDtypeStruct((2, 1, 2, 8), F32),
            jax.ShapeDtypeStruct((3, 2, 1, 2, 8), F32),
            jax.ShapeDtypeStruct((2, 1, 2, 8, 9), F32),
        ),
        in_specs=[vmem],
        out_specs=(vmem,) * 3,
        name="finish",
    )(total)
    return energy, forces, jnp.transpose(virial, (4, 0, 1, 2, 3))


def solution(mesh):
    placed = (
        P(None, "gx", "gy", "gz", None),
        P("gx", "gy", "gz", None, None),
        P("gx", "gy", "gz", None),
        P(("gx", "gy", "gz")),
        P(("gx", "gy", "gz"), None),
        P(("gx", "gy", "gz")),
    ) + (P(),) * 9
    shape = tuple(mesh.shape[axis] for axis in ("gx", "gy", "gz"))
    return jax.shard_map(
        functools.partial(local, shape),
        mesh=mesh,
        in_specs=placed,
        out_specs=(
            P("gx", "gy", "gz", None),
            P(None, "gx", "gy", "gz", None),
            P(None, "gx", "gy", "gz", None),
        ),
        check_vma=False,
    )
```

```python
import functools
import math

import jax
import jax.numpy as jnp
import numpy as np
from jax import lax
from jax.experimental import pallas as pl
from jax.experimental.pallas import tpu as pltpu
from jax.sharding import PartitionSpec as P

MESH = pl.DeviceIdType.MESH
F32 = jnp.float32
BF16 = jnp.bfloat16
CUTOFF = 5.0
CELL_SIDE = 4.6
ROOT_HALF = 0.7071067811865476
CHANNELS = 128
PAIRS = 1024
DIRECTIONS = [(a, b, c) for a in (-1, 0, 1) for b in (-1, 0, 1) for c in (-1, 0, 1)]
HOME = 13
CHUNK = 1024


def offsets():
    steps = range(-2, 3)
    return [
        (i, j, k)
        for i in steps
        for j in steps
        for k in steps
        if 0 < i * i + j * j + k * k <= 4
    ]


@functools.cache
def pairs():
    result = []
    for own in range(32):
        cell, inner = divmod(own, 8)
        at = (2 + 2 * (cell // 2) + inner // 4, 2 + inner // 2 % 2, 2 + 2 * (cell % 2) + inner % 2)
        for step in offsets():
            place = tuple(u + v for u, v in zip(at, step))
            site = place[0] % 2 * 4 + place[1] % 2 * 2 + place[2] % 2
            cx, cy, cz = (u // 2 for u in place)
            row = ((cx * 3 + cy) * 4 + cz) * 8 + site
            toward_x = -1 if cx == 0 else int(cx == 3)
            toward_z = -1 if cz == 0 else int(cz == 3)
            direction = (toward_x + 1) * 9 + cy * 3 + toward_z + 1
            near_cell = (cx - 1 - 2 * toward_x) * 2 + (cz - 1 - 2 * toward_z)
            shift = [CELL_SIDE * (u // 2 - v // 2) for u, v in zip(place, at)]
            result.append((own, row, direction, near_cell * 8 + site, shift))
    return result


@functools.cache
def wanted():
    slots = [sorted({p[3] for p in pairs() if p[2] == i}) for i in range(27)]
    slots[HOME] = list(range(32))
    order = [HOME] + sorted(
        (i for i in range(27) if i != HOME),
        key=lambda i: (sum(map(bool, DIRECTIONS[i])), i),
    )
    starts, row = {}, 0
    for i in order:
        starts[i] = row
        row += len(slots[i])
    return slots, starts, order


def receiving():
    slots, _, _ = wanted()
    return [sorted({slot // 8 for slot in slots[26 - i]}) for i in range(27)]


@functools.cache
def tables():
    slots, starts, _ = wanted()
    near = np.array([starts[p[2]] + slots[p[2]].index(p[3]) for p in pairs()])
    own = np.array([p[0] for p in pairs()])
    direction = np.array([p[2] for p in pairs()])
    slot = np.array([p[3] for p in pairs()])
    lane = np.arange(128)
    shift = np.zeros((8, PAIRS), np.float32)
    shift[:3] = np.array([p[4] for p in pairs()]).T
    cells = receiving()
    rank = np.array([cells[26 - i].index(j // 8) for i, j in zip(direction, slot)])
    column = np.concatenate([direction * 4 + rank, HOME * 4 + own // 8])
    site = np.concatenate([slot % 8, own % 8])
    return dict(
        gather=(near[:, None] == np.arange(256)[None]).astype(jnp.bfloat16),
        scatter=(np.arange(112)[:, None] == column[None]).astype(jnp.bfloat16),
        pick=np.concatenate(
            [lane[:, None] % 32 == slot[None], lane[:, None] % 32 == own[None]], axis=0
        ).astype(jnp.bfloat16),
        from_domain=(direction[None] == np.arange(32)[:, None]).astype(np.float32),
        sites=(np.arange(8)[:, None] == site[None]).astype(np.float32),
        shift=shift,
        listed=np.array([p[1] for p in pairs()]).reshape(32, 32).astype(np.int32),
    )


def mul(a, b):
    return lax.dot_general(a, b, (((1,), (0,)), ((), ())), preferred_element_type=F32)


def mul_t(a, b):
    return lax.dot_general(a, b, (((1,), (1,)), ((), ())), preferred_element_type=F32)


def split(a):
    high = a.astype(BF16)
    return high, (a - high.astype(F32)).astype(BF16)


def split3(a):
    high = a.astype(BF16)
    rest = a - high.astype(F32)
    mid = rest.astype(BF16)
    return high, mid, (rest - mid.astype(F32)).astype(BF16)


def iota(shape, axis):
    return lax.broadcasted_iota(jnp.int32, shape, axis)


def halves(a):
    return a[:, :CHANNELS] + a[:, CHANNELS:]


def beside(*parts):
    return jnp.concatenate(parts, axis=1)


def above(*parts):
    return jnp.concatenate(parts, axis=0)


def stack_of(high, low):
    return above(beside(high, low), beside(high, jnp.zeros_like(low)))


def project(rows, weight):
    return halves(mul(beside(*split(rows)), stack_of(*split(weight))))


def position_row(positions):
    repeat = (iota((8, 128), 0) == iota((8, 128), 1) % 8).astype(F32).astype(BF16)
    spread = sum(mul(part, repeat) for part in split3(positions))
    own = iota((12, 128), 1) // 8 == iota((12, 128), 0)
    return jnp.sum(jnp.where(own, spread, 0.0), axis=0, keepdims=True)


def by_component(rows):
    lanes = iota(rows.shape, 1) // 32
    return above(*[jnp.where(lanes == axis, rows, 0.0) for axis in range(3)])


def listed_pairs(centers, neighbours, listed):
    names = (centers == iota((32, 32), 0)).astype(F32)
    occupied = jnp.sum(names, axis=1, keepdims=True)
    name_bits = names.astype(BF16)
    entries = neighbours.astype(F32)
    coarse = jnp.floor(entries * (1.0 / 32.0))
    fine = entries - 32.0 * coarse
    by_slot = 32.0 * mul(name_bits, coarse.astype(BF16)) + mul(name_bits, fine.astype(BF16))
    wanted = listed.astype(F32)
    found = jnp.zeros((32, 32), F32)
    for entry in range(32):
        found = jnp.where(by_slot[:, entry : entry + 1] == wanted, 1.0, found)
    found = found * occupied
    spread_out = (iota((32, PAIRS), 1) % 32 == iota((32, PAIRS), 0)).astype(F32).astype(BF16)
    wide = mul(found.astype(BF16), spread_out)
    own = iota((32, PAIRS), 1) // 32 == iota((32, PAIRS), 0)
    return jnp.sum(jnp.where(own, wide, 0.0), axis=0, keepdims=True), occupied


def sine_cosine(ratio):
    angle = (ratio - 0.5) * math.pi
    square = angle * angle
    sine, cosine = jnp.zeros_like(ratio), jnp.zeros_like(ratio)
    for k in range(6, -1, -1):
        sign = (-1.0) ** k
        cosine = cosine * square + sign / math.factorial(2 * k)
        if k < 6:
            sine = sine * square + sign / math.factorial(2 * k + 1)
    return cosine, -sine * angle


def multiples(sine, cosine):
    s, c = {1: sine}, {1: cosine}
    for m in range(2, 9):
        if m % 2 == 0:
            h = m // 2
            s[m] = 2.0 * s[h] * c[h]
            c[m] = 1.0 - 2.0 * s[h] * s[h]
        else:
            a, b = m // 2, m - m // 2
            s[m] = s[a] * c[b] + c[a] * s[b]
            c[m] = c[a] * c[b] - s[a] * s[b]
    order = range(1, 9)
    return above(*[s[m] for m in order]), above(*[c[m] for m in order])


def geometry(displace, live):
    dx = jnp.where(live > 0.0, displace[0:1], 6.0)
    dy = jnp.where(live > 0.0, displace[1:2], 0.0)
    dz = jnp.where(live > 0.0, displace[2:3], 0.0)
    length = jnp.sqrt(dx * dx + dy * dy + dz * dz)
    inverse = 1.0 / length
    ratio = length * (1.0 / CUTOFF)
    square = ratio * ratio
    fourth = square * square
    inside = ratio < 1.0
    weight = 1.0 + fourth * square * (-28.0 + ratio * (48.0 - 21.0 * ratio))
    weight = jnp.where(inside, weight, 0.0) * live
    gap = 1.0 - ratio
    slope = jnp.where(inside, (-168.0 / CUTOFF) * fourth * ratio * gap * gap, 0.0) * live
    frequency = (iota((8, PAIRS), 0) + 1).astype(F32) * math.pi
    sines, cosines = multiples(*sine_cosine(jnp.minimum(ratio, 1.0)))
    scale = math.sqrt(2.0 / CUTOFF)
    basis = scale * sines * inverse
    basis_slope = (scale / CUTOFF * frequency * cosines - basis) * inverse
    ex, ey, ez = dx * inverse, dy * inverse, dz * inverse
    three, fifteen, five = math.sqrt(3.0), math.sqrt(15.0), math.sqrt(5.0)
    angular = above(
        three * ex,
        three * ey,
        three * ez,
        fifteen * ex * ey,
        fifteen * ey * ez,
        0.5 * five * (3.0 * ez * ez - 1.0),
        fifteen * ex * ez,
        0.5 * fifteen * (ex * ex - ey * ey),
    )
    return dict(
        d=(dx, dy, dz), e=(ex, ey, ez), inverse=inverse, weight=weight, slope=slope,
        basis=basis, basis_slope=basis_slope, angular=angular,
    )


def pair_gradient(geo, grad_basis, grad_weight, grad_angular):
    ex, ey, ez = geo["e"]
    three, fifteen, five = math.sqrt(3.0), math.sqrt(15.0), math.sqrt(5.0)
    g = [None] + [grad_angular[m : m + 1] for m in range(8)]
    radial = grad_weight * geo["slope"] + jnp.sum(
        grad_basis * geo["basis_slope"], axis=0, keepdims=True
    )
    ux = three * g[1] + fifteen * (g[4] * ey + g[7] * ez + g[8] * ex)
    uy = three * g[2] + fifteen * (g[4] * ex + g[5] * ez - g[8] * ey)
    uz = three * g[3] + fifteen * (g[5] * ey + g[7] * ex) + 3.0 * five * g[6] * ez
    along = radial - geo["inverse"] * (ux * ex + uy * ey + uz * ez)
    return tuple(along * e + geo["inverse"] * u for e, u in zip((ex, ey, ez), (ux, uy, uz)))


def parcels(d, grad, sites, scatter):
    virial = [-0.5 * a * b for a in d for b in grad]
    near = [-g for g in grad] + virial
    home = list(grad) + virial
    near_sites, home_sites = sites[:, :PAIRS], sites[:, PAIRS:]
    stacked = beside(
        above(*[near_sites * part for part in near]),
        above(*[home_sites * part for part in home]),
    )
    high, low = split(stacked)
    zero = jnp.zeros((32, 2 * PAIRS), BF16)
    return halves(mul_t(scatter, above(high, zero, low, zero)))


def interactions(geo, near_rows, own_proj, pull_rows, gather, basis_weight, paths, weights, chunk):
    (value_high, value_low, latent_high, latent_low, latent_t_high, latent_t_low,
     value_t_high, value_t_low) = weights
    basis_high, basis_low = split(basis_weight)
    near_high, near_low = split(near_rows)
    table = above(
        beside(near_high, near_low),
        beside(basis_high, basis_low),
        beside(basis_high, jnp.zeros_like(basis_low)),
        jnp.zeros((32, 256), BF16),
    )
    readout = above(
        beside(basis_weight, jnp.zeros((8, CHANNELS), F32)),
        beside(jnp.zeros((8, CHANNELS), F32), jnp.ones((8, CHANNELS), F32)),
    )
    readout_high, readout_low = split(readout)
    value_both = above(value_high, value_high)
    latent_both = beside(latent_high, latent_low)
    latent_t_both = above(latent_t_high, latent_t_high)
    value_t_both = beside(value_t_high, value_t_low)
    of_center = [
        (iota((8, 256), 1) // 32 == t).astype(F32) for t in range(8)
    ]
    ones = (iota((8, 256), 1) // 32 == iota((8, 256), 0)).astype(F32)
    basis_top = geo["basis"].astype(BF16).astype(F32)
    basis_rest = geo["basis"] - basis_top
    lane = iota((256, 128), 1)
    sums, grad_scalars, grad_angulars = [], [], []
    per = chunk // 256
    spare = jnp.zeros((56, 256), BF16)

    def stacked_paths(high, low):
        return above(
            beside(high, low), spare, beside(high, jnp.zeros_like(low)), spare
        )

    for first in range(0, 4, per):
        blocks = range(first, first + per)
        ys, y_ts, us, lefts = [], [], [], []
        for block in blocks:
            at = slice(block * 256, block * 256 + 256)
            angular = geo["angular"][:, at]
            y = above(*[angular * of_center[t] for t in range(8)], ones)
            flat = jnp.transpose(
                above(
                    y,
                    jnp.zeros((8, 256), F32),
                    basis_top[:, at],
                    basis_rest[:, at],
                    jnp.broadcast_to(geo["weight"][:, at], (8, 256)),
                    jnp.zeros((24, 256), F32),
                )
            )
            ys.append(split(y))
            y_ts.append(beside(*split(jnp.where(lane < 72, flat, 0.0))))
            us.append(jnp.broadcast_to(flat[:, 96:97], (256, 128)))
            radial = jnp.where((lane >= 80) & (lane < 96), flat, 0.0).astype(BF16)
            lefts.append(beside(gather[at, :128], gather[at, 128:] + radial))
        u = above(*us)
        h = halves(mul(above(*lefts), table)) + own_rows(own_proj, blocks)
        gate = jax.nn.sigmoid(h)
        silu = h * gate
        latent = u * silu
        l_high, l_low = split(latent)
        mixed = mul(beside(l_high, l_low), value_both) + mul(l_high, value_low)
        value, env = mixed[:, :128], mixed[:, 128:]
        env_high, env_low = split(env)
        inners, path_parts = [], []
        for k, block in enumerate(blocks):
            at = slice(k * 256, k * 256 + 256)
            y_high, y_low = ys[k]
            gamma = halves(mul(y_high, beside(env_high[at], env_low[at])))
            gamma = gamma + mul(y_low, env_high[at])
            parts = split(paths * gamma)
            path_parts.append(parts)
            inners.append(halves(mul(y_ts[k], stacked_paths(*parts))))
        inner = above(*inners)
        s_high, s_low = split(value * inner)
        q = halves(mul(beside(l_high, s_high), latent_both))
        q = q + mul(beside(l_low, s_low), latent_high)
        q_gate = jax.nn.sigmoid(q)
        update = q * q_gate
        sums.append(jnp.sum((latent + u * update).reshape(8 * per, 32, CHANNELS), axis=1))
        pull = own_rows(pull_rows, blocks)
        grad_q = u * pull * (q_gate * (1.0 + q - update))
        g_high, g_low = split(grad_q)
        grad_joined = mul(beside(g_high, g_low), latent_t_both) + mul(g_high, latent_t_low)
        grad_scalar = grad_joined[:, 128:]
        i_high, i_low = split(grad_scalar * value)
        v_high, v_low = split(grad_scalar * inner)
        grad_envs = []
        for k, block in enumerate(blocks):
            at = slice(k * 256, k * 256 + 256)
            y_high, y_low = ys[k]
            grad_path = halves(mul(y_high, beside(i_high[at], i_low[at])))
            grad_path = grad_path + mul(y_low, i_high[at])
            c_high, c_low = split(paths * grad_path)
            grad_envs.append(halves(mul(y_ts[k], stacked_paths(c_high, c_low))))
            path_high, path_low = path_parts[k]
            left_high = beside(path_high[:64], c_high[:64])
            left_low = beside(path_low[:64], c_low[:64])
            both = beside(i_high[at], env_high[at])
            cross = mul_t(above(left_high, left_low), both)
            cross = cross[:64] + cross[64:]
            cross = cross + mul_t(left_high, beside(i_low[at], env_low[at]))
            total = cross[0:8] * of_center[0]
            for t in range(1, 8):
                total = total + cross[8 * t : 8 * t + 8] * of_center[t]
            grad_angulars.append(total)
        e_high, e_low = split(above(*grad_envs))
        grad_latent = pull + grad_joined[:, :128]
        grad_latent = grad_latent + halves(mul(beside(v_high, e_high), value_t_both))
        grad_latent = grad_latent + mul(beside(v_low, e_low), value_t_high)
        grad_h = grad_latent * u * (gate * (1.0 + h - silu))
        grad_u = pull * update + grad_latent * silu
        h_high, h_low = split(grad_h)
        u_high, u_low = split(grad_u)
        both = mul_t(above(readout_high, readout_low), beside(h_high, u_high))
        grad_scalars.append(
            both[:16] + both[16:] + mul_t(readout_high, beside(h_low, u_low))
        )
    return above(*sums), beside(*grad_scalars), beside(*grad_angulars)


def own_rows(ref, blocks):
    return above(
        *[
            jnp.broadcast_to(ref[pl.ds(block * 8 + t, 1), :], (32, CHANNELS))
            for block in blocks
            for t in range(8)
        ]
    )


def path_rows(path_weight, scale):
    row = iota((72, CHANNELS), 0)
    first, second, third = (path_weight[i : i + 1] for i in range(3))
    return jnp.where(row >= 64, first, jnp.where(row % 8 < 3, second, third)) * scale


def of_kind(species, table):
    result = jnp.zeros(species.shape, F32)
    for kind in range(5):
        result = jnp.where(species == kind, table[0:1, kind : kind + 1], result)
    return result


def column_of(cells):
    rows = above(*[jnp.broadcast_to(cells[i : i + 1], (8, 8)) for i in range(4)])
    own = iota((32, 8), 0) % 8 == iota((32, 8), 1)
    return jnp.sum(jnp.where(own, rows, 0), axis=1, keepdims=True)


def kernel(
    shape,
    positions_hbm, features_hbm, near_hbm,
    species_hbm, centers_hbm, neighbours_hbm, scale_hbm, shift_hbm,
    center_hbm, basis_hbm, path_hbm, value_hbm, latent_hbm, out_hbm,
    listed_hbm, cell_shift_hbm, gather_hbm, scatter_hbm, pick_hbm, domain_hbm, sites_hbm,
    result_ref,
    positions_w, own_w, near_w,
    species_w, centers_w, neighbours_w, scale_w, shift_w,
    center_w, basis_w, path_w, value_w, latent_w, out_w,
    listed_v, cell_shift_v, gather_v, scatter_v, pick_v, domain_v, sites_v,
    mine, message, halo, few, places, returns, outgoing, proj_v, pull_v, ledger,
    local_sem, send_sem, recv_sem,
):
    me = tuple(lax.axis_index(axis) for axis in ("gx", "gy", "gz"))

    def device(direction):
        return tuple(
            lax.rem(i + step + size, size) for i, step, size in zip(me, direction, shape)
        )

    others = [(i, d) for i, d in enumerate(DIRECTIONS) if i != HOME]
    far_first = sorted(others, key=lambda item: -sum(map(abs, item[1])))
    barrier = pltpu.get_barrier_semaphore()
    for _, direction in far_first:
        pl.semaphore_signal(barrier, inc=1, device_id=device(direction), device_id_type=MESH)

    sources = (
        positions_hbm, features_hbm, near_hbm, species_hbm, centers_hbm, neighbours_hbm,
        scale_hbm, shift_hbm, center_hbm, basis_hbm, path_hbm, value_hbm, latent_hbm, out_hbm,
        listed_hbm, cell_shift_hbm, gather_hbm, scatter_hbm, pick_hbm, domain_hbm, sites_hbm,
    )
    targets = (
        positions_w, own_w, near_w, species_w, centers_w, neighbours_w,
        scale_w, shift_w, center_w, basis_w, path_w, value_w, latent_w, out_w,
        listed_v, cell_shift_v, gather_v, scatter_v, pick_v, domain_v, sites_v,
    )
    fetches = [
        pltpu.make_async_copy(src, dst, local_sem.at[i])
        for i, (src, dst) in enumerate(zip(sources, targets))
    ]
    for copy in fetches:
        copy.start()

    slots, starts, order = wanted()
    for copy in fetches[:3]:
        copy.wait()
    own = own_w[...].reshape(32, CHANNELS)
    mine[...] = project(own, near_w[...])
    place = position_row(positions_w[...].reshape(12, 8))
    places[...] = jnp.zeros_like(places)
    places[HOME : HOME + 1, :] = place
    for index, _ in others:
        taken = slots[26 - index]
        done = 0
        while done < len(taken):
            run = 1
            while done + run < len(taken) and taken[done + run] == taken[done] + run:
                run += 1
            message[index, done : done + run] = mine[taken[done] : taken[done] + run]
            done += run
        message[index, done : done + 1] = place
    pl.semaphore_wait(barrier, 26)

    for index, direction in far_first:
        rows = pl.ds(0, len(slots[26 - index]) + 1)
        pltpu.make_async_remote_copy(
            src_ref=message.at[index, rows],
            dst_ref=halo.at[26 - index, rows],
            send_sem=send_sem.at[0],
            recv_sem=recv_sem.at[0],
            device_id=device(direction),
            device_id_type=MESH,
        ).start()

    def settle(rows, semaphore):
        ref = ledger.at[pl.ds(0, rows)]
        pltpu.make_async_copy(ref, ref, semaphore).wait()

    sent_rows = sum(len(slots[i]) + 1 for i, _ in others)

    for copy in fetches[3:]:
        copy.wait()
    live, occupied = listed_pairs(centers_w[...], neighbours_w[...], listed_v[...])
    species = column_of(species_w[...].reshape(4, 8))
    scale = of_kind(species, scale_w[...])
    shift = of_kind(species, shift_w[...])
    pull_v[...] = occupied * scale * out_w[...] * (ROOT_HALF / math.sqrt(32.0))
    proj_v[...] = project(own, center_w[...])
    own_place = sum(mul(part, pick_v[128:256]) for part in split3(by_component(place)))
    base = cell_shift_v[0:3] - own_place[0:3]
    value, latent = value_w[...], latent_w[...]
    weights = (
        split(value) + split(latent) + split(jnp.transpose(latent)) + split(jnp.transpose(value))
    )
    paths = path_rows(path_w[...], 1.0 / math.sqrt(32.0))

    settle(sent_rows, recv_sem.at[0])

    for index, _ in others:
        count = len(slots[index])
        places[index : index + 1, :] = halo[index, count : count + 1]
        if count < 16:
            start = starts[index] - 160
            few[start : start + count, :] = halo[index, 0:count]
    near_rows = above(
        mine[...], *[halo[i, 0 : len(slots[i])] for i in order[1:7]], few[...]
    )
    gathered = sum(mul(part, pick_v[0:128]) for part in split3(by_component(places[...])))
    chosen = above(
        *[
            jnp.sum(gathered[32 * i : 32 * i + 32] * domain_v[...], axis=0, keepdims=True)
            for i in range(3)
        ]
    )
    geo = geometry(chosen + base, live)
    sums, grad_scalars, grad_angular = interactions(
        geo, near_rows, proj_v, pull_v, gather_v, basis_w[...], paths, weights, CHUNK
    )
    grad = pair_gradient(geo, grad_scalars[0:8], grad_scalars[8:9], grad_angular)
    owed = parcels(geo["d"], grad, sites_v[...], scatter_v[...])
    for index in range(27):
        outgoing[index, 0:4] = owed[4 * index : 4 * index + 4]

    cells = receiving()
    for index, direction in far_first:
        rows = pl.ds(0, len(cells[26 - index]))
        pltpu.make_async_remote_copy(
            src_ref=outgoing.at[index, rows],
            dst_ref=returns.at[26 - index, rows],
            send_sem=send_sem.at[1],
            recv_sem=recv_sem.at[1],
            device_id=device(direction),
            device_id_type=MESH,
        ).start()

    energy = jnp.sum(sums * out_w[...], axis=1, keepdims=True) * (ROOT_HALF / math.sqrt(32.0))
    energy = occupied * (scale * energy + shift)
    at_lane = iota((32, 128), 1) == 96 + iota((32, 128), 0) % 8
    energies = jnp.sum(jnp.where(at_lane, energy, 0.0).reshape(4, 8, 128), axis=1)
    totals = [outgoing[HOME, cell : cell + 1] + energies[cell : cell + 1] for cell in range(4)]
    returned_rows = sum(len(cells[i]) for i, _ in others)
    settle(sent_rows, send_sem.at[0])
    settle(returned_rows, recv_sem.at[1])
    for index, _ in others:
        for row, cell in enumerate(cells[index]):
            totals[cell] = totals[cell] + returns[index, row : row + 1]
    result_ref[...] = above(*totals, jnp.zeros((4, 128), F32))
    settle(returned_rows, send_sem.at[1])


def finish(total_ref, energy_ref, forces_ref, virial_ref):
    total = total_ref[0:4, :]
    energy = total[:, 96:104]
    for cx in range(2):
        energy_ref[cx, 0] = energy[2 * cx : 2 * cx + 2]
    for component in range(3):
        piece = total[:, component * 8 : component * 8 + 8]
        for cx in range(2):
            forces_ref[component, cx, 0] = piece[2 * cx : 2 * cx + 2]
    rows = above(*[jnp.broadcast_to(total[i : i + 1], (8, 128)) for i in range(4)])
    rows = jnp.where(iota((32, 128), 1) % 8 == iota((32, 128), 0) % 8, rows, 0.0)
    fold = (iota((128, 128), 0) // 8 - 3 == iota((128, 128), 1)).astype(F32).astype(BF16)
    by_site = sum(mul(part, fold) for part in split3(rows))
    for cell in range(4):
        virial_ref[cell // 2, 0, cell % 2] = by_site[8 * cell : 8 * cell + 8, 0:9]


def local(shape, *arguments):
    (positions, features, species, centers, neighbours, _, species_scale, species_shift,
     center_weight, near_weight, basis_weight, path_weight, value_weight, latent_weight,
     out_weight) = arguments
    fixed = {name: jnp.asarray(value) for name, value in tables().items()}
    vmem = pl.BlockSpec(memory_space=pltpu.VMEM)
    operands = (
        positions, features, near_weight,
        species, centers.reshape(1, 32), neighbours, species_scale.reshape(1, 5),
        species_shift.reshape(1, 5), center_weight, basis_weight, path_weight, value_weight,
        latent_weight, out_weight.reshape(1, 128),
        fixed["listed"], fixed["shift"], fixed["gather"], fixed["scatter"], fixed["pick"],
        fixed["from_domain"], fixed["sites"],
    )
    total = pl.pallas_call(
        functools.partial(kernel, shape),
        out_shape=pltpu.VMEM((8, 128), F32),
        in_specs=[pl.BlockSpec(memory_space=pltpu.HBM)] * len(operands),
        out_specs=vmem,
        scratch_shapes=[pltpu.VMEM(x.shape, x.dtype) for x in operands]
        + [
            pltpu.VMEM((32, CHANNELS), F32),
            pltpu.VMEM((27, 40, CHANNELS), F32),
            pltpu.VMEM((27, 40, CHANNELS), F32),
            pltpu.VMEM((48, CHANNELS), F32),
            pltpu.VMEM((32, 128), F32),
            pltpu.VMEM((27, 8, 128), F32),
            pltpu.VMEM((27, 8, 128), F32),
            pltpu.VMEM((32, CHANNELS), F32),
            pltpu.VMEM((32, CHANNELS), F32),
            pltpu.VMEM((208, 128), F32),
            pltpu.SemaphoreType.DMA((len(operands),)),
            pltpu.SemaphoreType.DMA((2,)),
            pltpu.SemaphoreType.DMA((2,)),
        ],
        compiler_params=pltpu.CompilerParams(
            collective_id=0,
            has_side_effects=True,
            vmem_limit_bytes=67030000,
        ),
        name="allegro",
    )(*operands)
    energy, forces, virial = pl.pallas_call(
        finish,
        out_shape=(
            jax.ShapeDtypeStruct((2, 1, 2, 8), F32),
            jax.ShapeDtypeStruct((3, 2, 1, 2, 8), F32),
            jax.ShapeDtypeStruct((2, 1, 2, 8, 9), F32),
        ),
        in_specs=[vmem],
        out_specs=(vmem,) * 3,
        compiler_params=pltpu.CompilerParams(vmem_limit_bytes=4 * 1024 * 1024),
        name="finish",
    )(total)
    return energy, forces, jnp.transpose(virial, (4, 0, 1, 2, 3))


def solution(mesh):
    placed = (
        P(None, "gx", "gy", "gz", None),
        P("gx", "gy", "gz", None, None),
        P("gx", "gy", "gz", None),
        P(("gx", "gy", "gz")),
        P(("gx", "gy", "gz"), None),
        P(("gx", "gy", "gz")),
    ) + (P(),) * 9
    shape = tuple(mesh.shape[axis] for axis in ("gx", "gy", "gz"))
    return jax.shard_map(
        functools.partial(local, shape),
        mesh=mesh,
        in_specs=placed,
        out_specs=(
            P("gx", "gy", "gz", None),
            P(None, "gx", "gy", "gz", None),
            P(None, "gx", "gy", "gz", None),
        ),
        check_vma=False,
    )
```

```python
import functools
import math

import jax
import jax.numpy as jnp
import numpy as np
from jax import lax
from jax.experimental import pallas as pl
from jax.experimental.pallas import tpu as pltpu
from jax.sharding import PartitionSpec as P

MESH = pl.DeviceIdType.MESH
F32 = jnp.float32
BF16 = jnp.bfloat16
CUTOFF = 5.0
CELL_SIDE = 4.6
ROOT_HALF = 0.7071067811865476
CHANNELS = 128
PAIRS = 1024
DIRECTIONS = [(a, b, c) for a in (-1, 0, 1) for b in (-1, 0, 1) for c in (-1, 0, 1)]
HOME = 13
CHUNKS = ((0,), (1, 2), (3,))


def offsets():
    steps = range(-2, 3)
    return [
        (i, j, k)
        for i in steps
        for j in steps
        for k in steps
        if 0 < i * i + j * j + k * k <= 4
    ]


@functools.cache
def own_order():
    def block(slot):
        x = slot // 16 * 2 + slot // 4 % 2
        z = slot // 8 % 2 * 2 + slot % 2
        outer_x, outer_z = x in (0, 3), z in (0, 3)
        return {(0, 0): 0, (1, 1): 1, (1, 0): 2, (0, 1): 3}[outer_x, outer_z]

    return sorted(range(32), key=lambda slot: (block(slot), slot))


@functools.cache
def pairs():
    result = []
    for own in own_order():
        cell, inner = divmod(own, 8)
        at = (2 + 2 * (cell // 2) + inner // 4, 2 + inner // 2 % 2, 2 + 2 * (cell % 2) + inner % 2)
        for step in offsets():
            place = tuple(u + v for u, v in zip(at, step))
            site = place[0] % 2 * 4 + place[1] % 2 * 2 + place[2] % 2
            cx, cy, cz = (u // 2 for u in place)
            row = ((cx * 3 + cy) * 4 + cz) * 8 + site
            toward_x = -1 if cx == 0 else int(cx == 3)
            toward_z = -1 if cz == 0 else int(cz == 3)
            direction = (toward_x + 1) * 9 + cy * 3 + toward_z + 1
            near_cell = (cx - 1 - 2 * toward_x) * 2 + (cz - 1 - 2 * toward_z)
            shift = [CELL_SIDE * (u // 2 - v // 2) for u, v in zip(place, at)]
            result.append((own, row, direction, near_cell * 8 + site, shift))
    return result


@functools.cache
def wanted():
    slots = [sorted({p[3] for p in pairs() if p[2] == i}) for i in range(27)]
    slots[HOME] = list(range(32))
    order = [HOME] + sorted(
        (i for i in range(27) if i != HOME),
        key=lambda i: (sum(map(bool, DIRECTIONS[i])), i),
    )
    starts, row = {}, 0
    for i in order:
        starts[i] = row
        row += len(slots[i])
    return slots, starts, order


def receiving():
    slots, _, _ = wanted()
    return [sorted({slot // 8 for slot in slots[26 - i]}) for i in range(27)]


@functools.cache
def tables():
    slots, starts, _ = wanted()
    near = np.array([starts[p[2]] + slots[p[2]].index(p[3]) for p in pairs()])
    own = np.array([p[0] for p in pairs()])
    direction = np.array([p[2] for p in pairs()])
    slot = np.array([p[3] for p in pairs()])
    lane = np.arange(128)
    shift = np.zeros((8, PAIRS), np.float32)
    shift[:3] = np.array([p[4] for p in pairs()]).T
    cells = receiving()
    rank = np.array([cells[26 - i].index(j // 8) for i, j in zip(direction, slot)])
    column = np.concatenate([direction * 4 + rank, HOME * 4 + own // 8])
    site = np.concatenate([slot % 8, own % 8])
    return dict(
        gather=(near[:, None] == np.arange(256)[None]).astype(jnp.bfloat16),
        scatter=(np.arange(112)[:, None] == column[None]).astype(jnp.bfloat16),
        pick=np.concatenate(
            [lane[:, None] % 32 == slot[None], lane[:, None] % 32 == own[None]], axis=0
        ).astype(jnp.bfloat16),
        from_domain=(direction[None] == np.arange(32)[:, None]).astype(np.float32),
        sites=(np.arange(8)[:, None] == site[None]).astype(np.float32),
        shift=shift,
        listed=np.concatenate(
            [np.array([p[1] for p in pairs()]).reshape(32, 32), own.reshape(32, 32)]
        ).astype(np.int32),
    )


def mul(a, b):
    return lax.dot_general(a, b, (((1,), (0,)), ((), ())), preferred_element_type=F32)


def mul_t(a, b):
    return lax.dot_general(a, b, (((1,), (1,)), ((), ())), preferred_element_type=F32)


def split(a):
    high = a.astype(BF16)
    return high, (a - high.astype(F32)).astype(BF16)


def split3(a):
    high = a.astype(BF16)
    rest = a - high.astype(F32)
    mid = rest.astype(BF16)
    return high, mid, (rest - mid.astype(F32)).astype(BF16)


def iota(shape, axis):
    return lax.broadcasted_iota(jnp.int32, shape, axis)


def halves(a):
    return a[:, :CHANNELS] + a[:, CHANNELS:]


def beside(*parts):
    return jnp.concatenate(parts, axis=1)


def above(*parts):
    return jnp.concatenate(parts, axis=0)


def stack_of(high, low):
    return above(beside(high, low), beside(high, jnp.zeros_like(low)))


def project(rows, weight):
    return halves(mul(beside(*split(rows)), stack_of(*split(weight))))


def position_row(positions):
    repeat = (iota((8, 128), 0) == iota((8, 128), 1) % 8).astype(F32).astype(BF16)
    spread = sum(mul(part, repeat) for part in split3(positions))
    own = iota((12, 128), 1) // 8 == iota((12, 128), 0)
    return jnp.sum(jnp.where(own, spread, 0.0), axis=0, keepdims=True)


def by_component(rows):
    lanes = iota(rows.shape, 1) // 32
    return above(*[jnp.where(lanes == axis, rows, 0.0) for axis in range(3)])


def listed_pairs(centers, neighbours, listed):
    slots = jnp.sum((centers == iota((32, 32), 0)).astype(F32), axis=1, keepdims=True)
    names = (centers == listed[32:]).astype(F32)
    occupied = jnp.sum(names, axis=1, keepdims=True)
    name_bits = names.astype(BF16)
    entries = neighbours.astype(F32)
    coarse = jnp.floor(entries * (1.0 / 32.0))
    fine = entries - 32.0 * coarse
    by_slot = 32.0 * mul(name_bits, coarse.astype(BF16)) + mul(name_bits, fine.astype(BF16))
    wanted = listed[:32].astype(F32)
    found = jnp.zeros((32, 32), F32)
    for entry in range(32):
        found = jnp.where(by_slot[:, entry : entry + 1] == wanted, 1.0, found)
    found = found * occupied
    spread_out = (iota((32, PAIRS), 1) % 32 == iota((32, PAIRS), 0)).astype(F32).astype(BF16)
    wide = mul(found.astype(BF16), spread_out)
    own = iota((32, PAIRS), 1) // 32 == iota((32, PAIRS), 0)
    return jnp.sum(jnp.where(own, wide, 0.0), axis=0, keepdims=True), slots


def sine_cosine(ratio):
    angle = (ratio - 0.5) * math.pi
    square = angle * angle
    sine, cosine = jnp.zeros_like(ratio), jnp.zeros_like(ratio)
    for k in range(6, -1, -1):
        sign = (-1.0) ** k
        cosine = cosine * square + sign / math.factorial(2 * k)
        if k < 6:
            sine = sine * square + sign / math.factorial(2 * k + 1)
    return cosine, -sine * angle


def multiples(sine, cosine):
    s, c = {1: sine}, {1: cosine}
    for m in range(2, 9):
        if m % 2 == 0:
            h = m // 2
            s[m] = 2.0 * s[h] * c[h]
            c[m] = 1.0 - 2.0 * s[h] * s[h]
        else:
            a, b = m // 2, m - m // 2
            s[m] = s[a] * c[b] + c[a] * s[b]
            c[m] = c[a] * c[b] - s[a] * s[b]
    order = range(1, 9)
    return above(*[s[m] for m in order]), above(*[c[m] for m in order])


def geometry(displace, live):
    dx = jnp.where(live > 0.0, displace[0:1], 6.0)
    dy = jnp.where(live > 0.0, displace[1:2], 0.0)
    dz = jnp.where(live > 0.0, displace[2:3], 0.0)
    length = jnp.sqrt(dx * dx + dy * dy + dz * dz)
    inverse = 1.0 / length
    ratio = length * (1.0 / CUTOFF)
    square = ratio * ratio
    fourth = square * square
    inside = ratio < 1.0
    weight = 1.0 + fourth * square * (-28.0 + ratio * (48.0 - 21.0 * ratio))
    weight = jnp.where(inside, weight, 0.0) * live
    gap = 1.0 - ratio
    slope = jnp.where(inside, (-168.0 / CUTOFF) * fourth * ratio * gap * gap, 0.0) * live
    frequency = (iota((8, live.shape[1]), 0) + 1).astype(F32) * math.pi
    sines, cosines = multiples(*sine_cosine(jnp.minimum(ratio, 1.0)))
    scale = math.sqrt(2.0 / CUTOFF)
    basis = scale * sines * inverse
    basis_slope = (scale / CUTOFF * frequency * cosines - basis) * inverse
    ex, ey, ez = dx * inverse, dy * inverse, dz * inverse
    three, fifteen, five = math.sqrt(3.0), math.sqrt(15.0), math.sqrt(5.0)
    angular = above(
        three * ex,
        three * ey,
        three * ez,
        fifteen * ex * ey,
        fifteen * ey * ez,
        0.5 * five * (3.0 * ez * ez - 1.0),
        fifteen * ex * ez,
        0.5 * fifteen * (ex * ex - ey * ey),
    )
    return dict(
        d=(dx, dy, dz), e=(ex, ey, ez), inverse=inverse, weight=weight, slope=slope,
        basis=basis, basis_slope=basis_slope, angular=angular,
    )


def pair_gradient(geo, grad_basis, grad_weight, grad_angular):
    ex, ey, ez = geo["e"]
    three, fifteen, five = math.sqrt(3.0), math.sqrt(15.0), math.sqrt(5.0)
    g = [None] + [grad_angular[m : m + 1] for m in range(8)]
    radial = grad_weight * geo["slope"] + jnp.sum(
        grad_basis * geo["basis_slope"], axis=0, keepdims=True
    )
    ux = three * g[1] + fifteen * (g[4] * ey + g[7] * ez + g[8] * ex)
    uy = three * g[2] + fifteen * (g[4] * ex + g[5] * ez - g[8] * ey)
    uz = three * g[3] + fifteen * (g[5] * ey + g[7] * ex) + 3.0 * five * g[6] * ez
    along = radial - geo["inverse"] * (ux * ex + uy * ey + uz * ez)
    return tuple(along * e + geo["inverse"] * u for e, u in zip((ex, ey, ez), (ux, uy, uz)))


def parcels(d, grad, sites, scatter):
    virial = [-0.5 * a * b for a in d for b in grad]
    near = [-g for g in grad] + virial
    home = list(grad) + virial
    count = d[0].shape[1]
    near_sites, home_sites = sites[:, :count], sites[:, count:]
    stacked = beside(
        above(*[near_sites * part for part in near]),
        above(*[home_sites * part for part in home]),
    )
    high, low = split(stacked)
    zero = jnp.zeros((32, 2 * count), BF16)
    return halves(mul_t(scatter, above(high, zero, low, zero)))


def near_table(near_rows, basis_weight):
    basis_high, basis_low = split(basis_weight)
    return above(
        beside(*split(near_rows)),
        beside(basis_high, basis_low),
        beside(basis_high, jnp.zeros_like(basis_low)),
        jnp.zeros((32, 256), BF16),
    )


def interactions(geo, table, own_proj, pull_rows, gather, basis_weight, paths, weights, blocks):
    (value_high, value_low, latent_high, latent_low, latent_t_high, latent_t_low,
     value_t_high, value_t_low) = weights
    readout = above(
        beside(basis_weight, jnp.zeros((8, CHANNELS), F32)),
        beside(jnp.zeros((8, CHANNELS), F32), jnp.ones((8, CHANNELS), F32)),
    )
    readout_high, readout_low = split(readout)
    value_both = above(value_high, value_high)
    latent_both = beside(latent_high, latent_low)
    latent_t_both = above(latent_t_high, latent_t_high)
    value_t_both = beside(value_t_high, value_t_low)
    of_center = [
        (iota((8, 256), 1) // 32 == t).astype(F32) for t in range(8)
    ]
    ones = (iota((8, 256), 1) // 32 == iota((8, 256), 0)).astype(F32)
    basis_top = geo["basis"].astype(BF16).astype(F32)
    basis_rest = geo["basis"] - basis_top
    lane = iota((256, 128), 1)
    sums, grad_scalars, grad_angulars = [], [], []
    per = len(blocks)
    spare = jnp.zeros((56, 256), BF16)

    def stacked_paths(high, low):
        return above(
            beside(high, low), spare, beside(high, jnp.zeros_like(low)), spare
        )

    ys, y_ts, us, lefts = [], [], [], []
    for k, block in enumerate(blocks):
        at = slice(k * 256, k * 256 + 256)
        rows = slice(block * 256, block * 256 + 256)
        angular = geo["angular"][:, at]
        y = above(*[angular * of_center[t] for t in range(8)], ones)
        flat = jnp.transpose(
            above(
                y,
                jnp.zeros((8, 256), F32),
                basis_top[:, at],
                basis_rest[:, at],
                jnp.broadcast_to(geo["weight"][:, at], (8, 256)),
                jnp.zeros((24, 256), F32),
            )
        )
        ys.append(split(y))
        y_ts.append(beside(*split(jnp.where(lane < 72, flat, 0.0))))
        us.append(jnp.broadcast_to(flat[:, 96:97], (256, 128)))
        radial = jnp.where((lane >= 80) & (lane < 96), flat, 0.0).astype(BF16)
        lefts.append(beside(gather[rows, :128], gather[rows, 128:] + radial))
    u = above(*us)
    h = halves(mul(above(*lefts), table)) + own_rows(own_proj, blocks)
    gate = jax.nn.sigmoid(h)
    silu = h * gate
    latent = u * silu
    l_high, l_low = split(latent)
    mixed = mul(beside(l_high, l_low), value_both) + mul(l_high, value_low)
    value, env = mixed[:, :128], mixed[:, 128:]
    env_high, env_low = split(env)
    inners, path_parts = [], []
    for k, block in enumerate(blocks):
        at = slice(k * 256, k * 256 + 256)
        y_high, y_low = ys[k]
        gamma = halves(mul(y_high, beside(env_high[at], env_low[at])))
        gamma = gamma + mul(y_low, env_high[at])
        parts = split(paths * gamma)
        path_parts.append(parts)
        inners.append(halves(mul(y_ts[k], stacked_paths(*parts))))
    inner = above(*inners)
    s_high, s_low = split(value * inner)
    q = halves(mul(beside(l_high, s_high), latent_both))
    q = q + mul(beside(l_low, s_low), latent_high)
    q_gate = jax.nn.sigmoid(q)
    update = q * q_gate
    sums.append(jnp.sum((latent + u * update).reshape(8 * per, 32, CHANNELS), axis=1))
    pull = own_rows(pull_rows, blocks)
    grad_q = u * pull * (q_gate * (1.0 + q - update))
    g_high, g_low = split(grad_q)
    grad_joined = mul(beside(g_high, g_low), latent_t_both) + mul(g_high, latent_t_low)
    grad_scalar = grad_joined[:, 128:]
    i_high, i_low = split(grad_scalar * value)
    v_high, v_low = split(grad_scalar * inner)
    grad_envs = []
    for k, block in enumerate(blocks):
        at = slice(k * 256, k * 256 + 256)
        y_high, y_low = ys[k]
        grad_path = halves(mul(y_high, beside(i_high[at], i_low[at])))
        grad_path = grad_path + mul(y_low, i_high[at])
        c_high, c_low = split(paths * grad_path)
        grad_envs.append(halves(mul(y_ts[k], stacked_paths(c_high, c_low))))
        path_high, path_low = path_parts[k]
        left_high = beside(path_high[:64], c_high[:64])
        left_low = beside(path_low[:64], c_low[:64])
        both = beside(i_high[at], env_high[at])
        cross = mul_t(above(left_high, left_low), both)
        cross = cross[:64] + cross[64:]
        cross = cross + mul_t(left_high, beside(i_low[at], env_low[at]))
        total = cross[0:8] * of_center[0]
        for t in range(1, 8):
            total = total + cross[8 * t : 8 * t + 8] * of_center[t]
        grad_angulars.append(total)
    e_high, e_low = split(above(*grad_envs))
    grad_latent = pull + grad_joined[:, :128]
    grad_latent = grad_latent + halves(mul(beside(v_high, e_high), value_t_both))
    grad_latent = grad_latent + mul(beside(v_low, e_low), value_t_high)
    grad_h = grad_latent * u * (gate * (1.0 + h - silu))
    grad_u = pull * update + grad_latent * silu
    h_high, h_low = split(grad_h)
    u_high, u_low = split(grad_u)
    both = mul_t(above(readout_high, readout_low), beside(h_high, u_high))
    grad_scalars.append(
        both[:16] + both[16:] + mul_t(readout_high, beside(h_low, u_low))
    )
    return above(*sums), beside(*grad_scalars), beside(*grad_angulars)


def own_rows(ref, blocks):
    return above(
        *[
            jnp.broadcast_to(ref[slot : slot + 1, :], (32, CHANNELS))
            for block in blocks
            for slot in own_order()[block * 8 : block * 8 + 8]
        ]
    )


def path_rows(path_weight, scale):
    row = iota((72, CHANNELS), 0)
    first, second, third = (path_weight[i : i + 1] for i in range(3))
    return jnp.where(row >= 64, first, jnp.where(row % 8 < 3, second, third)) * scale


def of_kind(species, table):
    result = jnp.zeros(species.shape, F32)
    for kind in range(5):
        result = jnp.where(species == kind, table[0:1, kind : kind + 1], result)
    return result


def column_of(cells):
    rows = above(*[jnp.broadcast_to(cells[i : i + 1], (8, 8)) for i in range(4)])
    own = iota((32, 8), 0) % 8 == iota((32, 8), 1)
    return jnp.sum(jnp.where(own, rows, 0), axis=1, keepdims=True)


def kernel(
    shape,
    positions_hbm, features_hbm, near_hbm,
    species_hbm, centers_hbm, neighbours_hbm, scale_hbm, shift_hbm,
    center_hbm, basis_hbm, path_hbm, value_hbm, latent_hbm, out_hbm,
    listed_hbm, cell_shift_hbm, gather_hbm, scatter_hbm, pick_hbm, domain_hbm, sites_hbm,
    result_ref,
    positions_w, own_w, near_w,
    species_w, centers_w, neighbours_w, scale_w, shift_w,
    center_w, basis_w, path_w, value_w, latent_w, out_w,
    listed_v, cell_shift_v, gather_v, scatter_v, pick_v, domain_v, sites_v,
    mine, message, halo, few, places, returns, outgoing, sums_v, proj_v, pull_v, ledger,
    local_sem, send_sem, recv_sem,
):
    me = tuple(lax.axis_index(axis) for axis in ("gx", "gy", "gz"))

    def device(direction):
        return tuple(
            lax.rem(i + step + size, size) for i, step, size in zip(me, direction, shape)
        )

    others = [(i, d) for i, d in enumerate(DIRECTIONS) if i != HOME]
    far_first = sorted(others, key=lambda item: -sum(map(abs, item[1])))
    barrier = pltpu.get_barrier_semaphore()
    for _, direction in far_first:
        pl.semaphore_signal(barrier, inc=1, device_id=device(direction), device_id_type=MESH)

    sources = (
        positions_hbm, features_hbm, near_hbm, species_hbm, centers_hbm, neighbours_hbm,
        scale_hbm, shift_hbm, center_hbm, basis_hbm, path_hbm, value_hbm, latent_hbm, out_hbm,
        listed_hbm, cell_shift_hbm, gather_hbm, scatter_hbm, pick_hbm, domain_hbm, sites_hbm,
    )
    targets = (
        positions_w, own_w, near_w, species_w, centers_w, neighbours_w,
        scale_w, shift_w, center_w, basis_w, path_w, value_w, latent_w, out_w,
        listed_v, cell_shift_v, gather_v, scatter_v, pick_v, domain_v, sites_v,
    )
    fetches = [
        pltpu.make_async_copy(src, dst, local_sem.at[i])
        for i, (src, dst) in enumerate(zip(sources, targets))
    ]
    for copy in fetches:
        copy.start()

    slots, starts, order = wanted()
    faces = order[1:7]
    for copy in fetches[:3]:
        copy.wait()
    own = own_w[...].reshape(32, CHANNELS)
    mine[...] = project(own, near_w[...])
    place = position_row(positions_w[...].reshape(12, 8))
    places[...] = jnp.zeros_like(places)
    places[HOME : HOME + 1, :] = place
    for index, _ in others:
        taken = slots[26 - index]
        done = 0
        while done < len(taken):
            run = 1
            while done + run < len(taken) and taken[done + run] == taken[done] + run:
                run += 1
            message[index, done : done + run] = mine[taken[done] : taken[done] + run]
            done += run
        message[index, done : done + 1] = place
    pl.semaphore_wait(barrier, 26)

    for index, direction in far_first:
        rows = pl.ds(0, len(slots[26 - index]) + 1)
        pltpu.make_async_remote_copy(
            src_ref=message.at[index, rows],
            dst_ref=halo.at[26 - index, rows],
            send_sem=send_sem.at[0],
            recv_sem=recv_sem.at[0 if index in faces else 1],
            device_id=device(direction),
            device_id_type=MESH,
        ).start()

    def settle(rows, semaphore):
        ref = ledger.at[pl.ds(0, rows)]
        pltpu.make_async_copy(ref, ref, semaphore).wait()

    sent_rows = sum(len(slots[i]) + 1 for i, _ in others)
    face_rows = sum(len(slots[i]) + 1 for i in faces)

    for copy in fetches[3:]:
        copy.wait()
    live, occupied = listed_pairs(centers_w[...], neighbours_w[...], listed_v[...])
    species = column_of(species_w[...].reshape(4, 8))
    scale = of_kind(species, scale_w[...])
    shift = of_kind(species, shift_w[...])
    pull_v[...] = occupied * scale * out_w[...] * (ROOT_HALF / math.sqrt(32.0))
    proj_v[...] = project(own, center_w[...])
    own_place = sum(mul(part, pick_v[128:256]) for part in split3(by_component(place)))
    base = cell_shift_v[0:3] - own_place[0:3]
    value, latent = value_w[...], latent_w[...]
    weights = (
        split(value) + split(latent) + split(jnp.transpose(latent)) + split(jnp.transpose(value))
    )
    paths = path_rows(path_w[...], 1.0 / math.sqrt(32.0))

    cells = receiving()

    def work(blocks, few_rows):
        columns = slice(blocks[0] * 256, blocks[-1] * 256 + 256)
        parts = split3(by_component(places[...]))
        gathered = sum(mul(part, pick_v[0:128, columns]) for part in parts)
        chosen = above(
            *[
                jnp.sum(
                    gathered[32 * i : 32 * i + 32] * domain_v[:, columns], axis=0, keepdims=True
                )
                for i in range(3)
            ]
        )
        geo = geometry(chosen + base[:, columns], live[:, columns])
        near_rows = above(mine[...], *[halo[i, 0 : len(slots[i])] for i in faces], few_rows)
        sums, grad_scalars, grad_angular = interactions(
            geo, near_table(near_rows, basis_w[...]), proj_v, pull_v, gather_v, basis_w[...],
            paths, weights, blocks,
        )
        for row, slot in enumerate(own_order()[blocks[0] * 8 : blocks[-1] * 8 + 8]):
            sums_v[slot : slot + 1, :] = sums[row : row + 1]
        grad = pair_gradient(geo, grad_scalars[0:8], grad_scalars[8:9], grad_angular)
        after = slice(PAIRS + columns.start, PAIRS + columns.stop)
        return parcels(
            geo["d"],
            grad,
            beside(sites_v[:, columns], sites_v[:, after]),
            beside(scatter_v[:, columns], scatter_v[:, after]),
        )

    def return_to(directions, owed):
        for index, _ in directions:
            outgoing[index, 0:4] = owed[4 * index : 4 * index + 4]
        for index, direction in directions:
            rows = pl.ds(0, len(cells[26 - index]))
            pltpu.make_async_remote_copy(
                src_ref=outgoing.at[index, rows],
                dst_ref=returns.at[26 - index, rows],
                send_sem=send_sem.at[1],
                recv_sem=recv_sem.at[2],
                device_id=device(direction),
                device_id_type=MESH,
            ).start()

    settle(face_rows, recv_sem.at[0])
    for index in faces:
        places[index : index + 1, :] = halo[index, len(slots[index]) : len(slots[index]) + 1]
    owed = work(CHUNKS[0], jnp.zeros((48, CHANNELS), F32))
    settle(sent_rows - face_rows, recv_sem.at[1])
    for index, _ in others:
        if index not in faces:
            count = len(slots[index])
            places[index : index + 1, :] = halo[index, count : count + 1]
            start = starts[index] - 160
            few[start : start + count, :] = halo[index, 0:count]
    early = [(i, d) for i, d in far_first if d[0] != 0 and (d[1] != 0 or d[2] != 0)]
    late = [item for item in far_first if item not in early]
    owed = owed + work(CHUNKS[1], few[...])
    return_to(early, owed)
    owed = owed + work(CHUNKS[2], few[...])
    return_to(late, owed)
    own_owed = owed[4 * HOME : 4 * HOME + 4]

    energy = jnp.sum(sums_v[...] * out_w[...], axis=1, keepdims=True) * (ROOT_HALF / math.sqrt(32.0))
    energy = occupied * (scale * energy + shift)
    at_lane = iota((32, 128), 1) == 96 + iota((32, 128), 0) % 8
    energies = jnp.sum(jnp.where(at_lane, energy, 0.0).reshape(4, 8, 128), axis=1)
    totals = [own_owed[cell : cell + 1] + energies[cell : cell + 1] for cell in range(4)]
    returned_rows = sum(len(cells[i]) for i, _ in others)
    settle(sent_rows, send_sem.at[0])
    settle(returned_rows, recv_sem.at[2])
    for index, _ in others:
        for row, cell in enumerate(cells[index]):
            totals[cell] = totals[cell] + returns[index, row : row + 1]
    result_ref[...] = above(*totals, jnp.zeros((4, 128), F32))
    settle(returned_rows, send_sem.at[1])


def finish(total_ref, energy_ref, forces_ref, virial_ref):
    total = total_ref[0:4, :]
    energy = total[:, 96:104]
    for cx in range(2):
        energy_ref[cx, 0] = energy[2 * cx : 2 * cx + 2]
    for component in range(3):
        piece = total[:, component * 8 : component * 8 + 8]
        for cx in range(2):
            forces_ref[component, cx, 0] = piece[2 * cx : 2 * cx + 2]
    rows = above(*[jnp.broadcast_to(total[i : i + 1], (8, 128)) for i in range(4)])
    rows = jnp.where(iota((32, 128), 1) % 8 == iota((32, 128), 0) % 8, rows, 0.0)
    fold = (iota((128, 128), 0) // 8 - 3 == iota((128, 128), 1)).astype(F32).astype(BF16)
    by_site = sum(mul(part, fold) for part in split3(rows))
    for cell in range(4):
        virial_ref[cell // 2, 0, cell % 2] = by_site[8 * cell : 8 * cell + 8, 0:9]


def local(shape, *arguments):
    (positions, features, species, centers, neighbours, _, species_scale, species_shift,
     center_weight, near_weight, basis_weight, path_weight, value_weight, latent_weight,
     out_weight) = arguments
    fixed = {name: jnp.asarray(value) for name, value in tables().items()}
    vmem = pl.BlockSpec(memory_space=pltpu.VMEM)
    operands = (
        positions, features, near_weight,
        species, centers.reshape(1, 32), neighbours, species_scale.reshape(1, 5),
        species_shift.reshape(1, 5), center_weight, basis_weight, path_weight, value_weight,
        latent_weight, out_weight.reshape(1, 128),
        fixed["listed"], fixed["shift"], fixed["gather"], fixed["scatter"], fixed["pick"],
        fixed["from_domain"], fixed["sites"],
    )
    total = pl.pallas_call(
        functools.partial(kernel, shape),
        out_shape=pltpu.VMEM((8, 128), F32),
        in_specs=[pl.BlockSpec(memory_space=pltpu.HBM)] * len(operands),
        out_specs=vmem,
        scratch_shapes=[pltpu.VMEM(x.shape, x.dtype) for x in operands]
        + [
            pltpu.VMEM((32, CHANNELS), F32),
            pltpu.VMEM((27, 40, CHANNELS), F32),
            pltpu.VMEM((27, 40, CHANNELS), F32),
            pltpu.VMEM((48, CHANNELS), F32),
            pltpu.VMEM((32, 128), F32),
            pltpu.VMEM((27, 8, 128), F32),
            pltpu.VMEM((27, 8, 128), F32),
            pltpu.VMEM((32, CHANNELS), F32),
            pltpu.VMEM((32, CHANNELS), F32),
            pltpu.VMEM((32, CHANNELS), F32),
            pltpu.VMEM((208, 128), F32),
            pltpu.SemaphoreType.DMA((len(operands),)),
            pltpu.SemaphoreType.DMA((2,)),
            pltpu.SemaphoreType.DMA((3,)),
        ],
        compiler_params=pltpu.CompilerParams(
            collective_id=0,
            has_side_effects=True,
            vmem_limit_bytes=67030000,
        ),
        name="allegro",
    )(*operands)
    energy, forces, virial = pl.pallas_call(
        finish,
        out_shape=(
            jax.ShapeDtypeStruct((2, 1, 2, 8), F32),
            jax.ShapeDtypeStruct((3, 2, 1, 2, 8), F32),
            jax.ShapeDtypeStruct((2, 1, 2, 8, 9), F32),
        ),
        in_specs=[vmem],
        out_specs=(vmem,) * 3,
        compiler_params=pltpu.CompilerParams(vmem_limit_bytes=4 * 1024 * 1024),
        name="finish",
    )(total)
    return energy, forces, jnp.transpose(virial, (4, 0, 1, 2, 3))


def solution(mesh):
    placed = (
        P(None, "gx", "gy", "gz", None),
        P("gx", "gy", "gz", None, None),
        P("gx", "gy", "gz", None),
        P(("gx", "gy", "gz")),
        P(("gx", "gy", "gz"), None),
        P(("gx", "gy", "gz")),
    ) + (P(),) * 9
    shape = tuple(mesh.shape[axis] for axis in ("gx", "gy", "gz"))
    return jax.shard_map(
        functools.partial(local, shape),
        mesh=mesh,
        in_specs=placed,
        out_specs=(
            P("gx", "gy", "gz", None),
            P(None, "gx", "gy", "gz", None),
            P(None, "gx", "gy", "gz", None),
        ),
        check_vma=False,
    )
```

```python
import functools
import math

import jax
import jax.numpy as jnp
import numpy as np
from jax import lax
from jax.experimental import pallas as pl
from jax.experimental.pallas import tpu as pltpu
from jax.sharding import PartitionSpec as P

MESH = pl.DeviceIdType.MESH
F32 = jnp.float32
BF16 = jnp.bfloat16
CUTOFF = 5.0
CELL_SIDE = 4.6
ROOT_HALF = 0.7071067811865476
CHANNELS = 128
PAIRS = 1024
DIRECTIONS = [(a, b, c) for a in (-1, 0, 1) for b in (-1, 0, 1) for c in (-1, 0, 1)]
HOME = 13
CHUNK = 512


def offsets():
    steps = range(-2, 3)
    return [
        (i, j, k)
        for i in steps
        for j in steps
        for k in steps
        if 0 < i * i + j * j + k * k <= 4
    ]


@functools.cache
def pairs():
    result = []
    for own in range(32):
        cell, inner = divmod(own, 8)
        at = (2 + 2 * (cell // 2) + inner // 4, 2 + inner // 2 % 2, 2 + 2 * (cell % 2) + inner % 2)
        for step in offsets():
            place = tuple(u + v for u, v in zip(at, step))
            site = place[0] % 2 * 4 + place[1] % 2 * 2 + place[2] % 2
            cx, cy, cz = (u // 2 for u in place)
            row = ((cx * 3 + cy) * 4 + cz) * 8 + site
            toward_x = -1 if cx == 0 else int(cx == 3)
            toward_z = -1 if cz == 0 else int(cz == 3)
            direction = (toward_x + 1) * 9 + cy * 3 + toward_z + 1
            near_cell = (cx - 1 - 2 * toward_x) * 2 + (cz - 1 - 2 * toward_z)
            shift = [CELL_SIDE * (u // 2 - v // 2) for u, v in zip(place, at)]
            result.append((own, row, direction, near_cell * 8 + site, shift))
    return result


@functools.cache
def wanted():
    slots = [sorted({p[3] for p in pairs() if p[2] == i}) for i in range(27)]
    slots[HOME] = list(range(32))
    order = [HOME] + sorted(
        (i for i in range(27) if i != HOME),
        key=lambda i: (sum(map(bool, DIRECTIONS[i])), i),
    )
    starts, row = {}, 0
    for i in order:
        starts[i] = row
        row += len(slots[i])
    return slots, starts, order


def receiving():
    slots, _, _ = wanted()
    return [sorted({slot // 8 for slot in slots[26 - i]}) for i in range(27)]


@functools.cache
def tables():
    slots, starts, _ = wanted()
    near = np.array([starts[p[2]] + slots[p[2]].index(p[3]) for p in pairs()])
    own = np.array([p[0] for p in pairs()])
    direction = np.array([p[2] for p in pairs()])
    slot = np.array([p[3] for p in pairs()])
    lane = np.arange(128)
    shift = np.zeros((8, PAIRS), np.float32)
    shift[:3] = np.array([p[4] for p in pairs()]).T
    cells = receiving()
    rank = np.array([cells[26 - i].index(j // 8) for i, j in zip(direction, slot)])
    column = direction * 4 + rank
    site = np.concatenate([slot % 8, own % 8])
    return dict(
        gather=(near[:, None] == np.arange(256)[None]).astype(jnp.bfloat16),
        scatter=np.concatenate(
            [np.arange(112)[:, None] == column[None], np.arange(16)[:, None] == own[None] // 8]
        ).astype(jnp.bfloat16),
        pick=np.concatenate(
            [lane[:, None] % 32 == slot[None], lane[:, None] % 32 == own[None]], axis=0
        ).astype(jnp.bfloat16),
        from_domain=(direction[None] == np.arange(32)[:, None]).astype(np.float32),
        sites=(np.arange(8)[:, None] == site[None]).astype(np.float32),
        shift=shift,
        listed=np.array([p[1] for p in pairs()]).reshape(32, 32).astype(np.int32),
    )


def mul(a, b):
    return lax.dot_general(a, b, (((1,), (0,)), ((), ())), preferred_element_type=F32)


def mul_t(a, b):
    return lax.dot_general(a, b, (((1,), (1,)), ((), ())), preferred_element_type=F32)


def split(a):
    high = a.astype(BF16)
    return high, (a - high.astype(F32)).astype(BF16)


def split3(a):
    high = a.astype(BF16)
    rest = a - high.astype(F32)
    mid = rest.astype(BF16)
    return high, mid, (rest - mid.astype(F32)).astype(BF16)


def iota(shape, axis):
    return lax.broadcasted_iota(jnp.int32, shape, axis)


def halves(a):
    return a[:, :CHANNELS] + a[:, CHANNELS:]


def beside(*parts):
    return jnp.concatenate(parts, axis=1)


def above(*parts):
    return jnp.concatenate(parts, axis=0)


def stack_of(high, low):
    return above(beside(high, low), beside(high, jnp.zeros_like(low)))


def project(rows, weight):
    return halves(mul(beside(*split(rows)), stack_of(*split(weight))))


def position_row(positions):
    repeat = (iota((8, 128), 0) == iota((8, 128), 1) % 8).astype(F32).astype(BF16)
    spread = sum(mul(part, repeat) for part in split3(positions))
    own = iota((12, 128), 1) // 8 == iota((12, 128), 0)
    return jnp.sum(jnp.where(own, spread, 0.0), axis=0, keepdims=True)


def by_component(rows):
    lanes = iota(rows.shape, 1) // 32
    return above(*[jnp.where(lanes == axis, rows, 0.0) for axis in range(3)])


def listed_pairs(centers, neighbours, listed):
    names = (centers == iota((32, 32), 0)).astype(F32)
    occupied = jnp.sum(names, axis=1, keepdims=True)
    name_bits = names.astype(BF16)
    entries = neighbours.astype(F32)
    coarse = jnp.floor(entries * (1.0 / 32.0))
    fine = entries - 32.0 * coarse
    by_slot = 32.0 * mul(name_bits, coarse.astype(BF16)) + mul(name_bits, fine.astype(BF16))
    wanted = listed.astype(F32)
    found = jnp.zeros((32, 32), F32)
    for entry in range(32):
        found = jnp.where(by_slot[:, entry : entry + 1] == wanted, 1.0, found)
    found = found * occupied
    spread_out = (iota((32, PAIRS), 1) % 32 == iota((32, PAIRS), 0)).astype(F32).astype(BF16)
    wide = mul(found.astype(BF16), spread_out)
    own = iota((32, PAIRS), 1) // 32 == iota((32, PAIRS), 0)
    return jnp.sum(jnp.where(own, wide, 0.0), axis=0, keepdims=True), occupied


def sine_cosine(ratio):
    angle = (ratio - 0.5) * math.pi
    square = angle * angle
    sine, cosine = jnp.zeros_like(ratio), jnp.zeros_like(ratio)
    for k in range(6, -1, -1):
        sign = (-1.0) ** k
        cosine = cosine * square + sign / math.factorial(2 * k)
        if k < 6:
            sine = sine * square + sign / math.factorial(2 * k + 1)
    return cosine, -sine * angle


def multiples(sine, cosine):
    s, c = {1: sine}, {1: cosine}
    for m in range(2, 9):
        if m % 2 == 0:
            h = m // 2
            s[m] = 2.0 * s[h] * c[h]
            c[m] = 1.0 - 2.0 * s[h] * s[h]
        else:
            a, b = m // 2, m - m // 2
            s[m] = s[a] * c[b] + c[a] * s[b]
            c[m] = c[a] * c[b] - s[a] * s[b]
    order = range(1, 9)
    return above(*[s[m] for m in order]), above(*[c[m] for m in order])


def geometry(displace, live):
    dx = jnp.where(live > 0.0, displace[0:1], 6.0)
    dy = jnp.where(live > 0.0, displace[1:2], 0.0)
    dz = jnp.where(live > 0.0, displace[2:3], 0.0)
    length = jnp.sqrt(dx * dx + dy * dy + dz * dz)
    inverse = 1.0 / length
    ratio = length * (1.0 / CUTOFF)
    square = ratio * ratio
    fourth = square * square
    inside = ratio < 1.0
    weight = 1.0 + fourth * square * (-28.0 + ratio * (48.0 - 21.0 * ratio))
    weight = jnp.where(inside, weight, 0.0) * live
    gap = 1.0 - ratio
    slope = jnp.where(inside, (-168.0 / CUTOFF) * fourth * ratio * gap * gap, 0.0) * live
    frequency = (iota((8, PAIRS), 0) + 1).astype(F32) * math.pi
    sines, cosines = multiples(*sine_cosine(jnp.minimum(ratio, 1.0)))
    scale = math.sqrt(2.0 / CUTOFF)
    basis = scale * sines * inverse
    basis_slope = (scale / CUTOFF * frequency * cosines - basis) * inverse
    ex, ey, ez = dx * inverse, dy * inverse, dz * inverse
    three, fifteen, five = math.sqrt(3.0), math.sqrt(15.0), math.sqrt(5.0)
    angular = above(
        three * ex,
        three * ey,
        three * ez,
        fifteen * ex * ey,
        fifteen * ey * ez,
        0.5 * five * (3.0 * ez * ez - 1.0),
        fifteen * ex * ez,
        0.5 * fifteen * (ex * ex - ey * ey),
    )
    return dict(
        d=(dx, dy, dz), e=(ex, ey, ez), inverse=inverse, weight=weight, slope=slope,
        basis=basis, basis_slope=basis_slope, angular=angular,
    )


def pair_gradient(geo, grad_basis, grad_weight, grad_angular):
    ex, ey, ez = geo["e"]
    three, fifteen, five = math.sqrt(3.0), math.sqrt(15.0), math.sqrt(5.0)
    g = [None] + [grad_angular[m : m + 1] for m in range(8)]
    radial = grad_weight * geo["slope"] + jnp.sum(
        grad_basis * geo["basis_slope"], axis=0, keepdims=True
    )
    ux = three * g[1] + fifteen * (g[4] * ey + g[7] * ez + g[8] * ex)
    uy = three * g[2] + fifteen * (g[4] * ex + g[5] * ez - g[8] * ey)
    uz = three * g[3] + fifteen * (g[5] * ey + g[7] * ex) + 3.0 * five * g[6] * ez
    along = radial - geo["inverse"] * (ux * ex + uy * ey + uz * ez)
    return tuple(along * e + geo["inverse"] * u for e, u in zip((ex, ey, ez), (ux, uy, uz)))


def owed_virial(d, grad):
    return [-0.5 * a * b for a in d for b in grad]


def parcels(terms, sites, scatter):
    high, low = split(above(*[sites * term for term in terms]))
    zero = jnp.zeros((32, PAIRS), BF16)
    return halves(mul_t(scatter, above(high, zero, low, zero)))


def interactions(geo, near_rows, own_proj, pull_rows, gather, basis_weight, paths, weights, chunk):
    (value_high, value_low, latent_high, latent_low, latent_t_high, latent_t_low,
     value_t_high, value_t_low) = weights
    basis_high, basis_low = split(basis_weight)
    near_high, near_low = split(near_rows)
    table = above(
        beside(near_high, near_low),
        beside(basis_high, basis_low),
        beside(basis_high, jnp.zeros_like(basis_low)),
        jnp.zeros((32, 256), BF16),
    )
    readout = above(
        beside(basis_weight, jnp.zeros((8, CHANNELS), F32)),
        beside(jnp.zeros((8, CHANNELS), F32), jnp.ones((8, CHANNELS), F32)),
    )
    readout_high, readout_low = split(readout)
    value_three = above(value_high, value_high, value_low)
    latent_both = beside(latent_high, latent_low)
    latent_t_three = above(latent_t_high, latent_t_high, latent_t_low)
    value_t_both = beside(value_t_high, value_t_low)
    of_center = [
        (iota((8, 256), 1) // 32 == t).astype(F32) for t in range(8)
    ]
    ones = (iota((8, 256), 1) // 32 == iota((8, 256), 0)).astype(F32)
    basis_top = geo["basis"].astype(BF16).astype(F32)
    basis_rest = geo["basis"] - basis_top
    lane = iota((256, 128), 1) + 128
    per = chunk // 256

    def parts_of(rows):
        high = rows.astype(BF16).astype(F32)
        return high, rows - high

    def stacked_paths(high, low):
        return above(high, high[:64], low, jnp.zeros((48, CHANNELS), F32)).astype(BF16)

    def gathered(y, high, low):
        both = mul(y, beside(high, low))
        top = halves(both[:72])
        return above(top[:64] + both[72:136, :CHANNELS], top[64:])

    results = {}

    def stages(blocks):
        ys, y_ts, us, lefts, angulars = [], [], [], [], []
        for block in blocks:
            at = slice(block * 256, block * 256 + 256)
            angular = geo["angular"][:, at]
            high, low = parts_of(above(*[angular * of_center[t] for t in range(8)]))
            high = above(high, ones)
            stack = above(
                high,
                low,
                high,
                basis_top[:, at],
                basis_rest[:, at],
                jnp.broadcast_to(geo["weight"][:, at], (8, 256)),
                jnp.zeros((24, 256), F32),
            )
            ys.append(stack[:144].astype(BF16))
            first_lanes, last_lanes = jnp.transpose(stack[:128]), jnp.transpose(stack[128:])
            y_ts.append(beside(first_lanes.astype(BF16), last_lanes.astype(BF16)))
            us.append(jnp.broadcast_to(last_lanes[:, 96:97], (256, 128)))
            radial = jnp.where((lane >= 208) & (lane < 224), last_lanes, 0.0).astype(BF16)
            lefts.append(beside(gather[at, :128], gather[at, 128:] + radial))
        u = above(*us)
        h = halves(mul(above(*lefts), table)) + own_rows(own_proj, blocks)
        yield
        gate = jax.nn.sigmoid(h)
        silu = h * gate
        latent = u * silu
        l_high, l_low = split(latent)
        mixed = mul(beside(l_high, l_low, l_high), value_three)
        yield
        value, env = mixed[:, :128], mixed[:, 128:]
        env_high, env_low = split(env)
        inners, path_parts = [], []
        for k, block in enumerate(blocks):
            at = slice(k * 256, k * 256 + 256)
            parts = parts_of(paths * gathered(ys[k], env_high[at], env_low[at]))
            path_parts.append(parts)
            inners.append(mul(y_ts[k], stacked_paths(*parts)))
        yield
        inner = above(*inners)
        s_high, s_low = split(value * inner)
        q = halves(mul(beside(l_high, s_high), latent_both))
        q = q + mul(beside(l_low, s_low), latent_high)
        yield
        q_gate = jax.nn.sigmoid(q)
        update = q * q_gate
        result_sums = (jnp.sum((latent + u * update).reshape(8 * per, 4, 8, CHANNELS), axis=1))
        pull = own_rows(pull_rows, blocks)
        grad_q = u * pull * (q_gate * (1.0 + q - update))
        g_high, g_low = split(grad_q)
        grad_joined = mul(beside(g_high, g_low, g_high), latent_t_three)
        yield
        grad_scalar = grad_joined[:, 128:]
        i_high, i_low = split(grad_scalar * value)
        v_high, v_low = split(grad_scalar * inner)
        grad_envs = []
        for k, block in enumerate(blocks):
            at = slice(k * 256, k * 256 + 256)
            c_high, c_low = parts_of(paths * gathered(ys[k], i_high[at], i_low[at]))
            grad_envs.append(mul(y_ts[k], stacked_paths(c_high, c_low)))
            path_high, path_low = path_parts[k]
            left_high = beside(path_high[:64], c_high[:64]).astype(BF16)
            left_low = beside(path_low[:64], c_low[:64]).astype(BF16)
            both = beside(i_high[at], env_high[at])
            cross = mul_t(above(left_high, left_low), both)
            cross = cross[:64] + cross[64:]
            cross = cross + mul_t(left_high, beside(i_low[at], env_low[at]))
            total = cross[0:8] * of_center[0]
            for t in range(1, 8):
                total = total + cross[8 * t : 8 * t + 8] * of_center[t]
            angulars.append(total)
        yield
        e_high, e_low = split(above(*grad_envs))
        grad_latent = pull + grad_joined[:, :128]
        grad_latent = grad_latent + halves(mul(beside(v_high, e_high), value_t_both))
        grad_latent = grad_latent + mul(beside(v_low, e_low), value_t_high)
        yield
        grad_h = grad_latent * u * (gate * (1.0 + h - silu))
        grad_u = pull * update + grad_latent * silu
        h_high, h_low = split(grad_h)
        u_high, u_low = split(grad_u)
        both = mul_t(above(readout_high, readout_low), beside(h_high, u_high))
        result_scalars = (
            both[:16] + both[16:] + mul_t(readout_high, beside(h_low, u_low))
        )
        results[blocks[0]] = (result_sums, result_scalars, beside(*angulars))
        yield

    running = [stages(range(i, i + per)) for i in range(0, 4, per)]
    for _ in range(8):
        for each in running:
            next(each)
    done = [results[i] for i in sorted(results)]
    return above(*[x[0] for x in done]), beside(*[x[1] for x in done]), beside(*[x[2] for x in done])


def own_rows(ref, blocks):
    return above(
        *[
            jnp.broadcast_to(ref[pl.ds(block * 8 + t, 1), :], (32, CHANNELS))
            for block in blocks
            for t in range(8)
        ]
    )


def path_rows(path_weight, scale):
    row = iota((72, CHANNELS), 0)
    first, second, third = (path_weight[i : i + 1] for i in range(3))
    return jnp.where(row >= 64, first, jnp.where(row % 8 < 3, second, third)) * scale


def of_kind(species, table):
    result = jnp.zeros(species.shape, F32)
    for kind in range(5):
        result = jnp.where(species == kind, table[0:1, kind : kind + 1], result)
    return result


def column_of(cells):
    rows = above(*[jnp.broadcast_to(cells[i : i + 1], (8, 8)) for i in range(4)])
    own = iota((32, 8), 0) % 8 == iota((32, 8), 1)
    return jnp.sum(jnp.where(own, rows, 0), axis=1, keepdims=True)


def kernel(
    shape,
    positions_hbm, features_hbm, near_hbm,
    species_hbm, centers_hbm, neighbours_hbm, scale_hbm, shift_hbm,
    center_hbm, basis_hbm, path_hbm, value_hbm, latent_hbm, out_hbm,
    listed_hbm, cell_shift_hbm, gather_hbm, scatter_hbm, pick_hbm, domain_hbm, sites_hbm,
    result_ref,
    positions_w, own_w, near_w,
    species_w, centers_w, neighbours_w, scale_w, shift_w,
    center_w, basis_w, path_w, value_w, latent_w, out_w,
    listed_v, cell_shift_v, gather_v, scatter_v, pick_v, domain_v, sites_v,
    mine, message, halo, few, places, returns, outgoing, sums_v, proj_v, pull_v, ledger,
    local_sem, send_sem, recv_sem,
):
    me = tuple(lax.axis_index(axis) for axis in ("gx", "gy", "gz"))

    def device(direction):
        return tuple(
            lax.rem(i + step + size, size) for i, step, size in zip(me, direction, shape)
        )

    others = [(i, d) for i, d in enumerate(DIRECTIONS) if i != HOME]
    far_first = sorted(others, key=lambda item: -sum(map(abs, item[1])))
    barrier = pltpu.get_barrier_semaphore()
    for _, direction in far_first:
        pl.semaphore_signal(barrier, inc=1, device_id=device(direction), device_id_type=MESH)

    sources = (
        positions_hbm, features_hbm, near_hbm, species_hbm, centers_hbm, neighbours_hbm,
        scale_hbm, shift_hbm, center_hbm, basis_hbm, path_hbm, value_hbm, latent_hbm, out_hbm,
        listed_hbm, cell_shift_hbm, gather_hbm, scatter_hbm, pick_hbm, domain_hbm, sites_hbm,
    )
    targets = (
        positions_w, own_w, near_w, species_w, centers_w, neighbours_w,
        scale_w, shift_w, center_w, basis_w, path_w, value_w, latent_w, out_w,
        listed_v, cell_shift_v, gather_v, scatter_v, pick_v, domain_v, sites_v,
    )
    fetches = [
        pltpu.make_async_copy(src, dst, local_sem.at[i])
        for i, (src, dst) in enumerate(zip(sources, targets))
    ]
    for copy in fetches:
        copy.start()

    slots, starts, order = wanted()
    for copy in fetches[:3]:
        copy.wait()
    own = own_w[...].reshape(32, CHANNELS)
    mine[...] = project(own, near_w[...])
    place = position_row(positions_w[...].reshape(12, 8))
    places[...] = jnp.zeros_like(places)
    places[HOME : HOME + 1, :] = place
    for index, _ in others:
        taken = slots[26 - index]
        done = 0
        while done < len(taken):
            run = 1
            while done + run < len(taken) and taken[done + run] == taken[done] + run:
                run += 1
            message[index, done : done + run] = mine[taken[done] : taken[done] + run]
            done += run
        message[index, done : done + 1] = place
    pl.semaphore_wait(barrier, 26)

    for index, direction in far_first:
        rows = pl.ds(0, len(slots[26 - index]) + 1)
        pltpu.make_async_remote_copy(
            src_ref=message.at[index, rows],
            dst_ref=halo.at[26 - index, rows],
            send_sem=send_sem.at[0],
            recv_sem=recv_sem.at[0],
            device_id=device(direction),
            device_id_type=MESH,
        ).start()

    def settle(rows, semaphore):
        ref = ledger.at[pl.ds(0, rows)]
        pltpu.make_async_copy(ref, ref, semaphore).wait()

    sent_rows = sum(len(slots[i]) + 1 for i, _ in others)

    for copy in fetches[3:]:
        copy.wait()
    live, occupied = listed_pairs(centers_w[...], neighbours_w[...], listed_v[...])
    species = column_of(species_w[...].reshape(4, 8))
    scale = of_kind(species, scale_w[...])
    shift = of_kind(species, shift_w[...])
    pull_v[...] = occupied * scale * out_w[...] * (ROOT_HALF / math.sqrt(32.0))
    proj_v[...] = project(own, center_w[...])
    own_place = sum(mul(part, pick_v[128:256]) for part in split3(by_component(place)))
    base = cell_shift_v[0:3] - own_place[0:3]
    value, latent = value_w[...], latent_w[...]
    weights = (
        split(value) + split(latent) + split(jnp.transpose(latent)) + split(jnp.transpose(value))
    )
    paths = path_rows(path_w[...], 1.0 / math.sqrt(32.0))

    settle(sent_rows, recv_sem.at[0])

    for index, _ in others:
        count = len(slots[index])
        places[index : index + 1, :] = halo[index, count : count + 1]
        if count < 16:
            start = starts[index] - 160
            few[start : start + count, :] = halo[index, 0:count]
    near_rows = above(
        mine[...], *[halo[i, 0 : len(slots[i])] for i in order[1:7]], few[...]
    )
    gathered = sum(mul(part, pick_v[0:128]) for part in split3(by_component(places[...])))
    chosen = above(
        *[
            jnp.sum(gathered[32 * i : 32 * i + 32] * domain_v[...], axis=0, keepdims=True)
            for i in range(3)
        ]
    )
    geo = geometry(chosen + base, live)
    sums_v[...], grad_scalars, grad_angular = interactions(
        geo, near_rows, proj_v, pull_v, gather_v, basis_w[...], paths, weights, CHUNK
    )
    grad = pair_gradient(geo, grad_scalars[0:8], grad_scalars[8:9], grad_angular)
    virial = owed_virial(geo["d"], grad)
    owed = parcels([-g for g in grad] + virial, sites_v[:, :PAIRS], scatter_v[0:112])
    for index, _ in others:
        outgoing[index, 0:4] = owed[4 * index : 4 * index + 4]

    cells = receiving()
    for index, direction in far_first:
        rows = pl.ds(0, len(cells[26 - index]))
        pltpu.make_async_remote_copy(
            src_ref=outgoing.at[index, rows],
            dst_ref=returns.at[26 - index, rows],
            send_sem=send_sem.at[1],
            recv_sem=recv_sem.at[1],
            device_id=device(direction),
            device_id_type=MESH,
        ).start()

    own_owed = parcels(list(grad) + virial, sites_v[:, PAIRS:], scatter_v[112:128])
    own_owed = own_owed[0:4] + owed[4 * HOME : 4 * HOME + 4]
    sums = jnp.sum(sums_v[...], axis=1)
    energy = jnp.sum(sums * out_w[...], axis=1, keepdims=True) * (ROOT_HALF / math.sqrt(32.0))
    energy = occupied * (scale * energy + shift)
    at_lane = iota((32, 128), 1) == 96 + iota((32, 128), 0) % 8
    energies = jnp.sum(jnp.where(at_lane, energy, 0.0).reshape(4, 8, 128), axis=1)
    totals = [own_owed[cell : cell + 1] + energies[cell : cell + 1] for cell in range(4)]
    returned_rows = sum(len(cells[i]) for i, _ in others)
    settle(sent_rows, send_sem.at[0])
    settle(returned_rows, recv_sem.at[1])
    for index, _ in others:
        for row, cell in enumerate(cells[index]):
            totals[cell] = totals[cell] + returns[index, row : row + 1]
    result_ref[...] = above(*totals, jnp.zeros((4, 128), F32))
    settle(returned_rows, send_sem.at[1])


def finish(total_ref, energy_ref, forces_ref, virial_ref):
    total = total_ref[0:4, :]
    energy = total[:, 96:104]
    for cx in range(2):
        energy_ref[cx, 0] = energy[2 * cx : 2 * cx + 2]
    for component in range(3):
        piece = total[:, component * 8 : component * 8 + 8]
        for cx in range(2):
            forces_ref[component, cx, 0] = piece[2 * cx : 2 * cx + 2]
    rows = above(*[jnp.broadcast_to(total[i : i + 1], (8, 128)) for i in range(4)])
    rows = jnp.where(iota((32, 128), 1) % 8 == iota((32, 128), 0) % 8, rows, 0.0)
    fold = (iota((128, 128), 0) // 8 - 3 == iota((128, 128), 1)).astype(F32).astype(BF16)
    by_site = sum(mul(part, fold) for part in split3(rows))
    for cell in range(4):
        virial_ref[cell // 2, 0, cell % 2] = by_site[8 * cell : 8 * cell + 8, 0:9]


def local(shape, *arguments):
    (positions, features, species, centers, neighbours, _, species_scale, species_shift,
     center_weight, near_weight, basis_weight, path_weight, value_weight, latent_weight,
     out_weight) = arguments
    fixed = {name: jnp.asarray(value) for name, value in tables().items()}
    vmem = pl.BlockSpec(memory_space=pltpu.VMEM)
    operands = (
        positions, features, near_weight,
        species, centers.reshape(1, 32), neighbours, species_scale.reshape(1, 5),
        species_shift.reshape(1, 5), center_weight, basis_weight, path_weight, value_weight,
        latent_weight, out_weight.reshape(1, 128),
        fixed["listed"], fixed["shift"], fixed["gather"], fixed["scatter"], fixed["pick"],
        fixed["from_domain"], fixed["sites"],
    )
    total = pl.pallas_call(
        functools.partial(kernel, shape),
        out_shape=pltpu.VMEM((8, 128), F32),
        in_specs=[pl.BlockSpec(memory_space=pltpu.HBM)] * len(operands),
        out_specs=vmem,
        scratch_shapes=[pltpu.VMEM(x.shape, x.dtype) for x in operands]
        + [
            pltpu.VMEM((32, CHANNELS), F32),
            pltpu.VMEM((27, 40, CHANNELS), F32),
            pltpu.VMEM((27, 40, CHANNELS), F32),
            pltpu.VMEM((48, CHANNELS), F32),
            pltpu.VMEM((32, 128), F32),
            pltpu.VMEM((27, 8, 128), F32),
            pltpu.VMEM((27, 8, 128), F32),
            pltpu.VMEM((32, 8, CHANNELS), F32),
            pltpu.VMEM((32, CHANNELS), F32),
            pltpu.VMEM((32, CHANNELS), F32),
            pltpu.VMEM((208, 128), F32),
            pltpu.SemaphoreType.DMA((len(operands),)),
            pltpu.SemaphoreType.DMA((2,)),
            pltpu.SemaphoreType.DMA((2,)),
        ],
        compiler_params=pltpu.CompilerParams(
            collective_id=0,
            has_side_effects=True,
            vmem_limit_bytes=67030000,
        ),
        name="allegro",
    )(*operands)
    energy, forces, virial = pl.pallas_call(
        finish,
        out_shape=(
            jax.ShapeDtypeStruct((2, 1, 2, 8), F32),
            jax.ShapeDtypeStruct((3, 2, 1, 2, 8), F32),
            jax.ShapeDtypeStruct((2, 1, 2, 8, 9), F32),
        ),
        in_specs=[vmem],
        out_specs=(vmem,) * 3,
        compiler_params=pltpu.CompilerParams(vmem_limit_bytes=4 * 1024 * 1024),
        name="finish",
    )(total)
    return energy, forces, jnp.transpose(virial, (4, 0, 1, 2, 3))


def solution(mesh):
    placed = (
        P(None, "gx", "gy", "gz", None),
        P("gx", "gy", "gz", None, None),
        P("gx", "gy", "gz", None),
        P(("gx", "gy", "gz")),
        P(("gx", "gy", "gz"), None),
        P(("gx", "gy", "gz")),
    ) + (P(),) * 9
    shape = tuple(mesh.shape[axis] for axis in ("gx", "gy", "gz"))
    return jax.shard_map(
        functools.partial(local, shape),
        mesh=mesh,
        in_specs=placed,
        out_specs=(
            P("gx", "gy", "gz", None),
            P(None, "gx", "gy", "gz", None),
            P(None, "gx", "gy", "gz", None),
        ),
        check_vma=False,
    )
```

```python
import functools
import math

import jax
import jax.numpy as jnp
import numpy as np
from jax import lax
from jax.experimental import pallas as pl
from jax.experimental.pallas import tpu as pltpu
from jax.sharding import PartitionSpec as P

MESH = pl.DeviceIdType.MESH
F32 = jnp.float32
BF16 = jnp.bfloat16
CUTOFF = 5.0
CELL_SIDE = 4.6
ROOT_HALF = 0.7071067811865476
CHANNELS = 128
PAIRS = 1024
DIRECTIONS = [(a, b, c) for a in (-1, 0, 1) for b in (-1, 0, 1) for c in (-1, 0, 1)]
HOME = 13
CHUNK = 512


def offsets():
    steps = range(-2, 3)
    return [
        (i, j, k)
        for i in steps
        for j in steps
        for k in steps
        if 0 < i * i + j * j + k * k <= 4
    ]


@functools.cache
def pairs():
    result = []
    for own in range(32):
        cell, inner = divmod(own, 8)
        at = (2 + 2 * (cell // 2) + inner // 4, 2 + inner // 2 % 2, 2 + 2 * (cell % 2) + inner % 2)
        for step in offsets():
            place = tuple(u + v for u, v in zip(at, step))
            site = place[0] % 2 * 4 + place[1] % 2 * 2 + place[2] % 2
            cx, cy, cz = (u // 2 for u in place)
            row = ((cx * 3 + cy) * 4 + cz) * 8 + site
            toward_x = -1 if cx == 0 else int(cx == 3)
            toward_z = -1 if cz == 0 else int(cz == 3)
            direction = (toward_x + 1) * 9 + cy * 3 + toward_z + 1
            near_cell = (cx - 1 - 2 * toward_x) * 2 + (cz - 1 - 2 * toward_z)
            shift = [CELL_SIDE * (u // 2 - v // 2) for u, v in zip(place, at)]
            result.append((own, row, direction, near_cell * 8 + site, shift))
    return result


@functools.cache
def wanted():
    slots = [sorted({p[3] for p in pairs() if p[2] == i}) for i in range(27)]
    slots[HOME] = list(range(32))
    order = [HOME] + sorted(
        (i for i in range(27) if i != HOME),
        key=lambda i: (sum(map(bool, DIRECTIONS[i])), i),
    )
    starts, row = {}, 0
    for i in order:
        starts[i] = row
        row += len(slots[i])
    return slots, starts, order


def receiving():
    slots, _, _ = wanted()
    return [sorted({slot // 8 for slot in slots[26 - i]}) for i in range(27)]


@functools.cache
def tables():
    slots, starts, _ = wanted()
    near = np.array([starts[p[2]] + slots[p[2]].index(p[3]) for p in pairs()])
    own = np.array([p[0] for p in pairs()])
    direction = np.array([p[2] for p in pairs()])
    slot = np.array([p[3] for p in pairs()])
    lane = np.arange(128)
    shift = np.zeros((8, PAIRS), np.float32)
    shift[:3] = np.array([p[4] for p in pairs()]).T
    cells = receiving()
    rank = np.array([cells[26 - i].index(j // 8) for i, j in zip(direction, slot)])
    column = direction * 4 + rank
    site = np.concatenate([slot % 8, own % 8])
    return dict(
        gather=(near[:, None] == np.arange(256)[None]).astype(jnp.bfloat16),
        scatter=np.concatenate(
            [np.arange(112)[:, None] == column[None], np.arange(16)[:, None] == own[None] // 8]
        ).astype(jnp.bfloat16),
        pick=np.concatenate(
            [lane[:, None] % 32 == slot[None], lane[:, None] % 32 == own[None]], axis=0
        ).astype(jnp.bfloat16),
        from_domain=(direction[None] == np.arange(32)[:, None]).astype(np.float32),
        sites=(np.arange(8)[:, None] == site[None]).astype(np.float32),
        shift=shift,
        listed=np.array([p[1] for p in pairs()]).reshape(32, 32).astype(np.int32),
    )


def mul(a, b):
    return lax.dot_general(a, b, (((1,), (0,)), ((), ())), preferred_element_type=F32)


def mul_t(a, b):
    return lax.dot_general(a, b, (((1,), (1,)), ((), ())), preferred_element_type=F32)


def split(a):
    high = a.astype(BF16)
    return high, (a - high.astype(F32)).astype(BF16)


def split3(a):
    high = a.astype(BF16)
    rest = a - high.astype(F32)
    mid = rest.astype(BF16)
    return high, mid, (rest - mid.astype(F32)).astype(BF16)


def mul_exact(rows, table):
    count = rows.shape[0]
    parts = mul(above(*split3(rows)), table)
    return parts[:count] + parts[count : 2 * count] + parts[2 * count :]


def iota(shape, axis):
    return lax.broadcasted_iota(jnp.int32, shape, axis)


def halves(a):
    return a[:, :CHANNELS] + a[:, CHANNELS:]


def beside(*parts):
    return jnp.concatenate(parts, axis=1)


def above(*parts):
    return jnp.concatenate(parts, axis=0)


def stack_of(high, low):
    return above(beside(high, low), beside(high, jnp.zeros_like(low)))


def project(rows, weight):
    return halves(mul(beside(*split(rows)), stack_of(*split(weight))))


def position_row(positions):
    repeat = (iota((8, 128), 0) == iota((8, 128), 1) % 8).astype(F32).astype(BF16)
    spread = sum(mul(part, repeat) for part in split3(positions))
    own = iota((12, 128), 1) // 8 == iota((12, 128), 0)
    return jnp.sum(jnp.where(own, spread, 0.0), axis=0, keepdims=True)


def by_component(rows):
    lanes = iota(rows.shape, 1) // 32
    return above(*[jnp.where(lanes == axis, rows, 0.0) for axis in range(3)])


def listed_pairs(centers, neighbours, listed):
    names = (centers == iota((32, 32), 0)).astype(F32)
    occupied = jnp.sum(names, axis=1, keepdims=True)
    name_bits = names.astype(BF16)
    entries = neighbours.astype(F32)
    coarse = jnp.floor(entries * (1.0 / 32.0))
    fine = entries - 32.0 * coarse
    by_slot = 32.0 * mul(name_bits, coarse.astype(BF16)) + mul(name_bits, fine.astype(BF16))
    wanted = listed.astype(F32)
    found = jnp.zeros((32, 32), F32)
    for entry in range(32):
        found = jnp.where(by_slot[:, entry : entry + 1] == wanted, 1.0, found)
    found = found * occupied
    spread_out = (iota((32, PAIRS), 1) % 32 == iota((32, PAIRS), 0)).astype(F32).astype(BF16)
    wide = mul(found.astype(BF16), spread_out)
    own = iota((32, PAIRS), 1) // 32 == iota((32, PAIRS), 0)
    return jnp.sum(jnp.where(own, wide, 0.0), axis=0, keepdims=True), occupied


def sine_cosine(ratio):
    angle = (ratio - 0.5) * math.pi
    square = angle * angle
    sine, cosine = jnp.zeros_like(ratio), jnp.zeros_like(ratio)
    for k in range(6, -1, -1):
        sign = (-1.0) ** k
        cosine = cosine * square + sign / math.factorial(2 * k)
        if k < 6:
            sine = sine * square + sign / math.factorial(2 * k + 1)
    return cosine, -sine * angle


def multiples(sine, cosine):
    s, c = {1: sine}, {1: cosine}
    for m in range(2, 9):
        if m % 2 == 0:
            h = m // 2
            s[m] = 2.0 * s[h] * c[h]
            c[m] = 1.0 - 2.0 * s[h] * s[h]
        else:
            a, b = m // 2, m - m // 2
            s[m] = s[a] * c[b] + c[a] * s[b]
            c[m] = c[a] * c[b] - s[a] * s[b]
    order = range(1, 9)
    return above(*[s[m] for m in order]), above(*[c[m] for m in order])


def geometry(displace, live):
    dx = jnp.where(live > 0.0, displace[0:1], 6.0)
    dy = jnp.where(live > 0.0, displace[1:2], 0.0)
    dz = jnp.where(live > 0.0, displace[2:3], 0.0)
    length = jnp.sqrt(dx * dx + dy * dy + dz * dz)
    inverse = 1.0 / length
    ratio = length * (1.0 / CUTOFF)
    square = ratio * ratio
    fourth = square * square
    inside = ratio < 1.0
    weight = 1.0 + fourth * square * (-28.0 + ratio * (48.0 - 21.0 * ratio))
    weight = jnp.where(inside, weight, 0.0) * live
    gap = 1.0 - ratio
    slope = jnp.where(inside, (-168.0 / CUTOFF) * fourth * ratio * gap * gap, 0.0) * live
    frequency = (iota((8, PAIRS), 0) + 1).astype(F32) * math.pi
    sines, cosines = multiples(*sine_cosine(jnp.minimum(ratio, 1.0)))
    scale = math.sqrt(2.0 / CUTOFF)
    basis = scale * sines * inverse
    basis_slope = (scale / CUTOFF * frequency * cosines - basis) * inverse
    ex, ey, ez = dx * inverse, dy * inverse, dz * inverse
    three, fifteen, five = math.sqrt(3.0), math.sqrt(15.0), math.sqrt(5.0)
    angular = above(
        three * ex,
        three * ey,
        three * ez,
        fifteen * ex * ey,
        fifteen * ey * ez,
        0.5 * five * (3.0 * ez * ez - 1.0),
        fifteen * ex * ez,
        0.5 * fifteen * (ex * ex - ey * ey),
    )
    return dict(
        d=(dx, dy, dz), e=(ex, ey, ez), inverse=inverse, weight=weight, slope=slope,
        basis=basis, basis_slope=basis_slope, angular=angular,
    )


def pair_gradient(geo, grad_basis, grad_weight, grad_angular):
    ex, ey, ez = geo["e"]
    three, fifteen, five = math.sqrt(3.0), math.sqrt(15.0), math.sqrt(5.0)
    g = [None] + [grad_angular[m : m + 1] for m in range(8)]
    radial = grad_weight * geo["slope"] + jnp.sum(
        grad_basis * geo["basis_slope"], axis=0, keepdims=True
    )
    ux = three * g[1] + fifteen * (g[4] * ey + g[7] * ez + g[8] * ex)
    uy = three * g[2] + fifteen * (g[4] * ex + g[5] * ez - g[8] * ey)
    uz = three * g[3] + fifteen * (g[5] * ey + g[7] * ex) + 3.0 * five * g[6] * ez
    along = radial - geo["inverse"] * (ux * ex + uy * ey + uz * ez)
    return tuple(along * e + geo["inverse"] * u for e, u in zip((ex, ey, ez), (ux, uy, uz)))


def owed_virial(d, grad):
    return [-0.5 * a * b for a in d for b in grad]


def parcels(terms, sites, scatter):
    high, low = split(above(*[sites * term for term in terms]))
    zero = jnp.zeros((32, PAIRS), BF16)
    return halves(mul_t(scatter, above(high, zero, low, zero)))


def interactions(geo, near_rows, own_proj, pull_rows, gather, basis_weight, paths, weights, chunk):
    (value_high, value_low, latent_high, latent_low, latent_t_high, latent_t_low,
     value_t_high, value_t_low) = weights
    basis_high, basis_low = split(basis_weight)
    near_high, near_low = split(near_rows)
    table = above(
        beside(near_high, near_low),
        beside(basis_high, basis_low),
        beside(basis_high, jnp.zeros_like(basis_low)),
        jnp.zeros((32, 256), BF16),
    )
    readout = above(
        beside(basis_weight, jnp.zeros((8, CHANNELS), F32)),
        beside(jnp.zeros((8, CHANNELS), F32), jnp.ones((8, CHANNELS), F32)),
    )
    readout_high, readout_low = split(readout)
    value_three = above(value_high, value_high, value_low)
    latent_both = beside(latent_high, latent_low)
    latent_t_three = above(latent_t_high, latent_t_high, latent_t_low)
    value_t_both = beside(value_t_high, value_t_low)
    of_center = [
        (iota((8, 256), 1) // 32 == t).astype(F32) for t in range(8)
    ]
    ones = (iota((8, 256), 1) // 32 == iota((8, 256), 0)).astype(F32)
    basis_top = geo["basis"].astype(BF16).astype(F32)
    basis_rest = geo["basis"] - basis_top
    lane = iota((256, 128), 1) + 128
    per = chunk // 256

    def parts_of(rows):
        high = rows.astype(BF16).astype(F32)
        return high, rows - high

    def stacked_paths(high, low):
        return above(high, high[:64], low, jnp.zeros((48, CHANNELS), F32)).astype(BF16)

    def gathered(y, high, low):
        both = mul(y, beside(high, low))
        top = halves(both[:72])
        return above(top[:64] + both[72:136, :CHANNELS], top[64:])

    results = {}

    def stages(blocks):
        ys, y_ts, us, lefts, angulars = [], [], [], [], []
        for block in blocks:
            at = slice(block * 256, block * 256 + 256)
            angular = geo["angular"][:, at]
            high, low = parts_of(above(*[angular * of_center[t] for t in range(8)]))
            high = above(high, ones)
            stack = above(
                high,
                low,
                high,
                basis_top[:, at],
                basis_rest[:, at],
                jnp.broadcast_to(geo["weight"][:, at], (8, 256)),
                jnp.zeros((24, 256), F32),
            )
            ys.append(stack[:144].astype(BF16))
            first_lanes, last_lanes = jnp.transpose(stack[:128]), jnp.transpose(stack[128:])
            y_ts.append(beside(first_lanes.astype(BF16), last_lanes.astype(BF16)))
            us.append(jnp.broadcast_to(last_lanes[:, 96:97], (256, 128)))
            radial = jnp.where((lane >= 208) & (lane < 224), last_lanes, 0.0).astype(BF16)
            lefts.append(beside(gather[at, :128], gather[at, 128:] + radial))
        u = above(*us)
        h = halves(mul(above(*lefts), table)) + own_rows(own_proj, blocks)
        yield
        gate = jax.nn.sigmoid(h)
        silu = h * gate
        latent = u * silu
        l_high, l_low = split(latent)
        mixed = mul(beside(l_high, l_low, l_high), value_three)
        yield
        value, env = mixed[:, :128], mixed[:, 128:]
        env_high, env_low = split(env)
        inners, path_parts = [], []
        for k, block in enumerate(blocks):
            at = slice(k * 256, k * 256 + 256)
            parts = parts_of(paths * gathered(ys[k], env_high[at], env_low[at]))
            path_parts.append(parts)
            inners.append(mul(y_ts[k], stacked_paths(*parts)))
        yield
        inner = above(*inners)
        s_high, s_low = split(value * inner)
        q = halves(mul(beside(l_high, s_high), latent_both))
        q = q + mul(beside(l_low, s_low), latent_high)
        yield
        q_gate = jax.nn.sigmoid(q)
        update = q * q_gate
        result_sums = (jnp.sum((latent + u * update).reshape(8 * per, 4, 8, CHANNELS), axis=1))
        pull = own_rows(pull_rows, blocks)
        grad_q = u * pull * (q_gate * (1.0 + q - update))
        g_high, g_low = split(grad_q)
        grad_joined = mul(beside(g_high, g_low, g_high), latent_t_three)
        yield
        grad_scalar = grad_joined[:, 128:]
        i_high, i_low = split(grad_scalar * value)
        v_high, v_low = split(grad_scalar * inner)
        grad_envs = []
        for k, block in enumerate(blocks):
            at = slice(k * 256, k * 256 + 256)
            c_high, c_low = parts_of(paths * gathered(ys[k], i_high[at], i_low[at]))
            grad_envs.append(mul(y_ts[k], stacked_paths(c_high, c_low)))
            path_high, path_low = path_parts[k]
            left_high = beside(path_high[:64], c_high[:64]).astype(BF16)
            left_low = beside(path_low[:64], c_low[:64]).astype(BF16)
            both = beside(i_high[at], env_high[at])
            cross = mul_t(above(left_high, left_low), both)
            cross = cross[:64] + cross[64:]
            cross = cross + mul_t(left_high, beside(i_low[at], env_low[at]))
            total = cross[0:8] * of_center[0]
            for t in range(1, 8):
                total = total + cross[8 * t : 8 * t + 8] * of_center[t]
            angulars.append(total)
        yield
        e_high, e_low = split(above(*grad_envs))
        grad_latent = pull + grad_joined[:, :128]
        grad_latent = grad_latent + halves(mul(beside(v_high, e_high), value_t_both))
        grad_latent = grad_latent + mul(beside(v_low, e_low), value_t_high)
        yield
        grad_h = grad_latent * u * (gate * (1.0 + h - silu))
        grad_u = pull * update + grad_latent * silu
        h_high, h_low = split(grad_h)
        u_high, u_low = split(grad_u)
        both = mul_t(above(readout_high, readout_low), beside(h_high, u_high))
        result_scalars = (
            both[:16] + both[16:] + mul_t(readout_high, beside(h_low, u_low))
        )
        results[blocks[0]] = (result_sums, result_scalars, beside(*angulars))
        yield

    running = [stages(range(i, i + per)) for i in range(0, 4, per)]
    for _ in range(8):
        for each in running:
            next(each)
    done = [results[i] for i in sorted(results)]
    return above(*[x[0] for x in done]), beside(*[x[1] for x in done]), beside(*[x[2] for x in done])


def own_rows(ref, blocks):
    return above(
        *[
            jnp.broadcast_to(ref[pl.ds(block * 8 + t, 1), :], (32, CHANNELS))
            for block in blocks
            for t in range(8)
        ]
    )


def path_rows(path_weight, scale):
    row = iota((72, CHANNELS), 0)
    first, second, third = (path_weight[i : i + 1] for i in range(3))
    return jnp.where(row >= 64, first, jnp.where(row % 8 < 3, second, third)) * scale


def of_kind(species, table):
    result = jnp.zeros(species.shape, F32)
    for kind in range(5):
        result = jnp.where(species == kind, table[0:1, kind : kind + 1], result)
    return result


def column_of(cells):
    rows = above(*[jnp.broadcast_to(cells[i : i + 1], (8, 8)) for i in range(4)])
    own = iota((32, 8), 0) % 8 == iota((32, 8), 1)
    return jnp.sum(jnp.where(own, rows, 0), axis=1, keepdims=True)


def kernel(
    shape,
    positions_hbm, features_hbm, near_hbm,
    species_hbm, centers_hbm, neighbours_hbm, scale_hbm, shift_hbm,
    center_hbm, basis_hbm, path_hbm, value_hbm, latent_hbm, out_hbm,
    listed_hbm, cell_shift_hbm, gather_hbm, scatter_hbm, pick_hbm, domain_hbm, sites_hbm,
    result_ref,
    positions_w, own_w, near_w,
    species_w, centers_w, neighbours_w, scale_w, shift_w,
    center_w, basis_w, path_w, value_w, latent_w, out_w,
    listed_v, cell_shift_v, gather_v, scatter_v, pick_v, domain_v, sites_v,
    mine, message, halo, few, places, returns, outgoing, sums_v, proj_v, pull_v, ledger,
    local_sem, send_sem, recv_sem,
):
    me = tuple(lax.axis_index(axis) for axis in ("gx", "gy", "gz"))

    def device(direction):
        return tuple(
            lax.rem(i + step + size, size) for i, step, size in zip(me, direction, shape)
        )

    others = [(i, d) for i, d in enumerate(DIRECTIONS) if i != HOME]
    far_first = sorted(others, key=lambda item: -sum(map(abs, item[1])))
    barrier = pltpu.get_barrier_semaphore()
    for _, direction in far_first:
        pl.semaphore_signal(barrier, inc=1, device_id=device(direction), device_id_type=MESH)

    sources = (
        positions_hbm, features_hbm, near_hbm, species_hbm, centers_hbm, neighbours_hbm,
        scale_hbm, shift_hbm, center_hbm, basis_hbm, path_hbm, value_hbm, latent_hbm, out_hbm,
        listed_hbm, cell_shift_hbm, gather_hbm, scatter_hbm, pick_hbm, domain_hbm, sites_hbm,
    )
    targets = (
        positions_w, own_w, near_w, species_w, centers_w, neighbours_w,
        scale_w, shift_w, center_w, basis_w, path_w, value_w, latent_w, out_w,
        listed_v, cell_shift_v, gather_v, scatter_v, pick_v, domain_v, sites_v,
    )
    fetches = [
        pltpu.make_async_copy(src, dst, local_sem.at[i])
        for i, (src, dst) in enumerate(zip(sources, targets))
    ]
    for copy in fetches:
        copy.start()

    slots, starts, order = wanted()
    for copy in fetches[:3]:
        copy.wait()
    own = own_w[...].reshape(32, CHANNELS)
    mine[...] = project(own, near_w[...])
    place = position_row(positions_w[...].reshape(12, 8))
    places[...] = jnp.zeros_like(places)
    places[HOME : HOME + 1, :] = place
    for index, _ in others:
        taken = slots[26 - index]
        done = 0
        while done < len(taken):
            run = 1
            while done + run < len(taken) and taken[done + run] == taken[done] + run:
                run += 1
            message[index, done : done + run] = mine[taken[done] : taken[done] + run]
            done += run
        message[index, done : done + 1] = place
    pl.semaphore_wait(barrier, 26)

    for index, direction in far_first:
        rows = pl.ds(0, len(slots[26 - index]) + 1)
        pltpu.make_async_remote_copy(
            src_ref=message.at[index, rows],
            dst_ref=halo.at[26 - index, rows],
            send_sem=send_sem.at[0],
            recv_sem=recv_sem.at[0],
            device_id=device(direction),
            device_id_type=MESH,
        ).start()

    def settle(rows, semaphore):
        ref = ledger.at[pl.ds(0, rows)]
        pltpu.make_async_copy(ref, ref, semaphore).wait()

    sent_rows = sum(len(slots[i]) + 1 for i, _ in others)

    for copy in fetches[3:]:
        copy.wait()
    live, occupied = listed_pairs(centers_w[...], neighbours_w[...], listed_v[...])
    species = column_of(species_w[...].reshape(4, 8))
    scale = of_kind(species, scale_w[...])
    shift = of_kind(species, shift_w[...])
    pull_v[...] = occupied * scale * out_w[...] * (ROOT_HALF / math.sqrt(32.0))
    proj_v[...] = project(own, center_w[...])
    own_place = sum(mul(part, pick_v[128:256]) for part in split3(by_component(place)))
    base = cell_shift_v[0:3] - own_place[0:3]
    value, latent = value_w[...], latent_w[...]
    weights = (
        split(value) + split(latent) + split(jnp.transpose(latent)) + split(jnp.transpose(value))
    )
    paths = path_rows(path_w[...], 1.0 / math.sqrt(32.0))

    settle(sent_rows, recv_sem.at[0])

    for index, _ in others:
        count = len(slots[index])
        places[index : index + 1, :] = halo[index, count : count + 1]
        if count < 16:
            start = starts[index] - 160
            few[start : start + count, :] = halo[index, 0:count]
    near_rows = above(
        mine[...], *[halo[i, 0 : len(slots[i])] for i in order[1:7]], few[...]
    )
    gathered = mul_exact(by_component(places[...]), pick_v[0:128])
    chosen = above(
        *[
            jnp.sum(gathered[32 * i : 32 * i + 32] * domain_v[...], axis=0, keepdims=True)
            for i in range(3)
        ]
    )
    geo = geometry(chosen + base, live)
    sums_v[...], grad_scalars, grad_angular = interactions(
        geo, near_rows, proj_v, pull_v, gather_v, basis_w[...], paths, weights, CHUNK
    )
    grad = pair_gradient(geo, grad_scalars[0:8], grad_scalars[8:9], grad_angular)
    virial = owed_virial(geo["d"], grad)
    owed = parcels([-g for g in grad] + virial, sites_v[:, :PAIRS], scatter_v[0:112])
    for index, _ in others:
        outgoing[index, 0:4] = owed[4 * index : 4 * index + 4]

    cells = receiving()
    for index, direction in far_first:
        rows = pl.ds(0, len(cells[26 - index]))
        pltpu.make_async_remote_copy(
            src_ref=outgoing.at[index, rows],
            dst_ref=returns.at[26 - index, rows],
            send_sem=send_sem.at[1],
            recv_sem=recv_sem.at[1],
            device_id=device(direction),
            device_id_type=MESH,
        ).start()

    own_owed = parcels(list(grad) + virial, sites_v[:, PAIRS:], scatter_v[112:128])
    own_owed = own_owed[0:4] + owed[4 * HOME : 4 * HOME + 4]
    sums = jnp.sum(sums_v[...], axis=1)
    energy = jnp.sum(sums * out_w[...], axis=1, keepdims=True) * (ROOT_HALF / math.sqrt(32.0))
    energy = occupied * (scale * energy + shift)
    at_lane = iota((32, 128), 1) == 96 + iota((32, 128), 0) % 8
    energies = jnp.sum(jnp.where(at_lane, energy, 0.0).reshape(4, 8, 128), axis=1)
    totals = [own_owed[cell : cell + 1] + energies[cell : cell + 1] for cell in range(4)]
    returned_rows = sum(len(cells[i]) for i, _ in others)
    settle(sent_rows, send_sem.at[0])
    settle(returned_rows, recv_sem.at[1])
    for index, _ in others:
        for row, cell in enumerate(cells[index]):
            totals[cell] = totals[cell] + returns[index, row : row + 1]
    result_ref[...] = above(*totals, jnp.zeros((4, 128), F32))
    settle(returned_rows, send_sem.at[1])


def finish(total_ref, energy_ref, forces_ref, virial_ref):
    total = total_ref[0:4, :]
    energy = total[:, 96:104]
    for cx in range(2):
        energy_ref[cx, 0] = energy[2 * cx : 2 * cx + 2]
    for component in range(3):
        piece = total[:, component * 8 : component * 8 + 8]
        for cx in range(2):
            forces_ref[component, cx, 0] = piece[2 * cx : 2 * cx + 2]
    rows = above(*[jnp.broadcast_to(total[i : i + 1], (8, 128)) for i in range(4)])
    rows = jnp.where(iota((32, 128), 1) % 8 == iota((32, 128), 0) % 8, rows, 0.0)
    fold = (iota((128, 128), 0) // 8 - 3 == iota((128, 128), 1)).astype(F32).astype(BF16)
    by_site = mul_exact(rows, fold)
    for cell in range(4):
        virial_ref[cell // 2, 0, cell % 2] = by_site[8 * cell : 8 * cell + 8, 0:9]


def local(shape, *arguments):
    (positions, features, species, centers, neighbours, _, species_scale, species_shift,
     center_weight, near_weight, basis_weight, path_weight, value_weight, latent_weight,
     out_weight) = arguments
    fixed = {name: jnp.asarray(value) for name, value in tables().items()}
    vmem = pl.BlockSpec(memory_space=pltpu.VMEM)
    operands = (
        positions, features, near_weight,
        species, centers.reshape(1, 32), neighbours, species_scale.reshape(1, 5),
        species_shift.reshape(1, 5), center_weight, basis_weight, path_weight, value_weight,
        latent_weight, out_weight.reshape(1, 128),
        fixed["listed"], fixed["shift"], fixed["gather"], fixed["scatter"], fixed["pick"],
        fixed["from_domain"], fixed["sites"],
    )
    total = pl.pallas_call(
        functools.partial(kernel, shape),
        out_shape=pltpu.VMEM((8, 128), F32),
        in_specs=[pl.BlockSpec(memory_space=pltpu.HBM)] * len(operands),
        out_specs=vmem,
        scratch_shapes=[pltpu.VMEM(x.shape, x.dtype) for x in operands]
        + [
            pltpu.VMEM((32, CHANNELS), F32),
            pltpu.VMEM((27, 40, CHANNELS), F32),
            pltpu.VMEM((27, 40, CHANNELS), F32),
            pltpu.VMEM((48, CHANNELS), F32),
            pltpu.VMEM((32, 128), F32),
            pltpu.VMEM((27, 8, 128), F32),
            pltpu.VMEM((27, 8, 128), F32),
            pltpu.VMEM((32, 8, CHANNELS), F32),
            pltpu.VMEM((32, CHANNELS), F32),
            pltpu.VMEM((32, CHANNELS), F32),
            pltpu.VMEM((208, 128), F32),
            pltpu.SemaphoreType.DMA((len(operands),)),
            pltpu.SemaphoreType.DMA((2,)),
            pltpu.SemaphoreType.DMA((2,)),
        ],
        compiler_params=pltpu.CompilerParams(
            collective_id=0,
            has_side_effects=True,
            vmem_limit_bytes=67030000,
        ),
        name="allegro",
    )(*operands)
    energy, forces, virial = pl.pallas_call(
        finish,
        out_shape=(
            jax.ShapeDtypeStruct((2, 1, 2, 8), F32),
            jax.ShapeDtypeStruct((3, 2, 1, 2, 8), F32),
            jax.ShapeDtypeStruct((2, 1, 2, 8, 9), F32),
        ),
        in_specs=[vmem],
        out_specs=(vmem,) * 3,
        compiler_params=pltpu.CompilerParams(vmem_limit_bytes=4 * 1024 * 1024),
        name="finish",
    )(total)
    return energy, forces, jnp.transpose(virial, (4, 0, 1, 2, 3))


def solution(mesh):
    placed = (
        P(None, "gx", "gy", "gz", None),
        P("gx", "gy", "gz", None, None),
        P("gx", "gy", "gz", None),
        P(("gx", "gy", "gz")),
        P(("gx", "gy", "gz"), None),
        P(("gx", "gy", "gz")),
    ) + (P(),) * 9
    shape = tuple(mesh.shape[axis] for axis in ("gx", "gy", "gz"))
    return jax.shard_map(
        functools.partial(local, shape),
        mesh=mesh,
        in_specs=placed,
        out_specs=(
            P("gx", "gy", "gz", None),
            P(None, "gx", "gy", "gz", None),
            P(None, "gx", "gy", "gz", None),
        ),
        check_vma=False,
    )
```
